32 devices in a mesh: section: 4 (over z), seq: 4 (over y, x), tp: 2 (over core).
Axes of the slice: x: 2, y: 2, z: 4, core: 2. Of those that a mesh axis runs over, the one named last changes fastest.
Arguments:
- queries: bfloat16 [4, 1024, 8192], P('section', 'seq', 'tp'), may hold values from -300 to 300
- vision: bfloat16 [128, 7680], P(('section', 'tp'), 'seq'), may hold values from -6 to 6
- kv_weight: bfloat16 [4, 7680, 2048], P('section', 'seq', 'tp'), may hold values from -0.0625 to 0.0625
- key_gain: float32 [4, 128], P('section'), may hold values from 0.25 to 1.75
- head_gate: float32 [4, 64], P('section', 'tp'), may hold values from -1.5 to 1.5
Outputs:
- attended: bfloat16 [4, 1024, 8192], P('section', 'seq', 'tp')
The draws below stay inside these ranges and needn't reach their ends.
All inputs are finite; a program needn't handle non-finite values.
Results may differ from the reference program's by a relative error of at most 0.01.
The reference program's roundings to bfloat16 on the way count: a program that leaves them out, or rounds other values in their place, can miss the bound.
Values may be sent and summed in bfloat16 or wider, within the bound.
A program may use at most 64 MiB of HBM per device.

```python
import jax
import jax.numpy as jnp
from jax import lax

DV = 7680
QH = 64
KVH = 8
HD = 128
SECTIONS = 4
TOKENS = 1024
V = 128


def draw_queries(key, part):
    base = jax.random.normal(key, (SECTIONS, TOKENS, QH * HD), jnp.float32)
    return jnp.clip(base, -6.0, 6.0).astype(jnp.bfloat16)


def steps_of(rng, dims, cuts, least, largest):
    factor_of, own = 1.0, jax.random.fold_in(rng, 6)
    for dim, shards_of in cuts:
        steps = jnp.exp(jax.random.uniform(jax.random.fold_in(own, dim), (shards_of,), jnp.float32, least / len(cuts), largest / len(cuts)))
        factor_of = factor_of * jnp.repeat(steps, dims[dim] // shards_of).reshape([-1 if axis == dim else 1 for axis in range(len(dims))])
    return factor_of


def noise(own_key, dims, width, most, pieces=(), kind=jnp.bfloat16):
    result = jax.random.normal(own_key, dims, jnp.float32) * width
    if len(pieces) > 0:
        result = steps_of(own_key, dims, pieces, -0.22, 0.18) * result
    return jnp.clip(result, min=-most, max=most).astype(kind)


def setup_inputs(seed: int = 0) -> dict:
    seeds = jax.random.split(jax.random.key(seed), 6)
    queries = draw_queries(jax.random.fold_in(seeds[5], 71), 0)
    vision = noise(seeds[1], (V, DV), 1.0, 6.0, ((0, 8), (1, 4)))
    kv_weight = noise(seeds[2], (SECTIONS, DV, KVH * 2 * HD), DV ** -0.5, 0.0625, ((0, 4), (1, 4), (2, 2)))
    key_gain = jnp.clip(1.0 + 0.15 * jax.random.normal(seeds[3], (SECTIONS, HD), jnp.float32), 0.25, 1.75)
    head_gate = jnp.clip(jax.random.uniform(seeds[4], (SECTIONS, QH), jnp.float32, -1.5, 1.5) * steps_of(seeds[4], (SECTIONS, QH), ((0, 4), (1, 2)), -0.4, 0.0), -1.5, 1.5)
    return {"queries": queries, "vision": vision, "kv_weight": kv_weight, "key_gain": key_gain, "head_gate": head_gate}


eps_norm = 1e-05

def key_values(vision, weights, gain):
    projected = jnp.dot(vision, weights, preferred_element_type=jnp.float32)
    rows = projected.shape[0]
    projected = projected.reshape(rows, KVH, 2, HD)
    keys_raw = projected[:, :, 0]
    values_raw = projected[:, :, 1]
    scaled = keys_raw * lax.rsqrt(lax.optimization_barrier(jnp.mean(keys_raw * keys_raw, axis=-1, keepdims=True)) + eps_norm) * gain
    return (scaled.astype(jnp.bfloat16), values_raw.astype(jnp.bfloat16))

def reference(queries, vision, kv_weight, key_gain, head_gate):
    group = QH // KVH

    def one_section(index):
        keys, values = key_values(vision, kv_weight[index], key_gain[index])
        grouped = queries[index].reshape(TOKENS, KVH, group, HD)

        def one_head(head):
            query_head = lax.dynamic_index_in_dim(grouped, head, 1, keepdims=False).astype(jnp.float32)
            key_head = lax.dynamic_index_in_dim(keys, head, 1, keepdims=False).astype(jnp.float32)
            value_head = lax.dynamic_index_in_dim(values, head, 1, keepdims=False).astype(jnp.float32)
            scores = jnp.einsum('tgd,rd->tgr', query_head, key_head, precision=lax.Precision.HIGHEST) * HD ** (-0.5)
            peak = lax.optimization_barrier(jnp.max(scores, axis=-1, keepdims=True))
            exp_scores = jnp.exp(scores - peak)
            total = lax.optimization_barrier(jnp.sum(exp_scores, axis=-1))
            rounded = lax.optimization_barrier(exp_scores.astype(jnp.bfloat16)).astype(jnp.float32)
            mixed = jnp.einsum('tgr,rd->tgd', rounded, value_head, precision=lax.Precision.HIGHEST)
            return mixed / total[..., None]
        heads = lax.map(one_head, jnp.arange(KVH, dtype=jnp.int32))
        heads = jnp.transpose(heads, (1, 0, 2, 3))
        gated = heads * jnp.tanh(head_gate[index]).reshape(1, KVH, group, 1)
        return gated.reshape(TOKENS, QH * HD).astype(jnp.bfloat16)
    return lax.map(one_section, jnp.arange(SECTIONS, dtype=jnp.int32))
```

```python
import functools

import jax
import jax.numpy as jnp
from jax import lax
from jax.experimental import pallas as pl
from jax.experimental.pallas import tpu as pltpu
from jax.sharding import PartitionSpec as P

MESH = pl.DeviceIdType.MESH
eps_norm = 1e-05


def project_kernel(
    sizes,
    head_dim,
    vision_ref,
    weight_ref,
    gain_ref,
    query_ref,
    key_ref,
    value_ref,
    staged_ref,
    seen,
    weights,
    gain,
    partial,
    landed,
    ready,
    gathered,
    load_sem,
    far_send,
    pass_send,
    seen_sem,
    sum_send,
    sum_recv,
    kv_send,
    kv_recv,
):
    n_s, n_q, n_t = sizes
    s, q, t = lax.axis_index("section"), lax.axis_index("seq"), lax.axis_index("tp")
    stages = partial.shape[0]
    per = n_s // stages
    half = n_s // 2 if n_s % 2 == 0 else n_s
    share = partial.shape[2]
    columns = partial.shape[3]
    heads = columns // (2 * head_dim)
    base = (s // half) * half

    def section_of(k):
        return lax.rem(base + (k // half) * half, n_s) + lax.rem(s + k, half)

    def place_at(k):
        return (k // half) * half + (half - k % half) % half

    others_s = [section_of(k) for k in range(1, n_s)]
    others_q = [lax.rem(q + k, n_q) for k in range(1, n_q)]
    others_t = [lax.rem(t + k, n_t) for k in range(1, n_t)]

    barrier = pltpu.get_barrier_semaphore()
    peers = (
        [(o, q, t) for o in others_s[::-1]]
        + [(s, o, t) for o in others_q]
        + [(s, q, o) for o in others_t]
    )
    for peer in peers:
        pl.semaphore_signal(barrier, inc=1, device_id=peer, device_id_type=MESH)
    own = pltpu.make_async_copy(vision_ref, seen.at[0, t], load_sem.at[0])
    own.start()
    load = pltpu.make_async_copy(weight_ref.at[0], weights, load_sem.at[1])
    load.start()
    load_gain = pltpu.make_async_copy(gain_ref, gain, load_sem.at[2])
    load_gain.start()
    stage_queries = pltpu.make_async_copy(query_ref, staged_ref, load_sem.at[3])
    stage_queries.start()
    own.wait()
    pl.semaphore_wait(barrier, len(peers))

    sent = []

    def send(src, dst, send_sem, recv_sem, peer):
        copy = pltpu.make_async_remote_copy(
            src_ref=src,
            dst_ref=dst,
            send_sem=send_sem,
            recv_sem=recv_sem,
            device_id=peer,
            device_id_type=MESH,
        )
        copy.start()
        sent.append(copy)

    def arrived(dst, sem):
        pltpu.make_async_copy(dst, dst, sem).wait()

    def pass_on(k):
        for i, o in enumerate(others_t):
            send(seen.at[k, t], seen.at[k, t], pass_send.at[k, i], seen_sem.at[k, t], (s, q, o))

    pass_on(0)
    for k, o in enumerate(others_s, 1):
        place = place_at(k)
        send(
            seen.at[0, t], seen.at[place, t], far_send.at[k - 1], seen_sem.at[place, t], (o, q, t)
        )
    load_gain.wait()
    load.wait()

    def project(stage):
        for k in range(stage * per, (stage + 1) * per):
            if k > 0:
                arrived(seen.at[k, t], seen_sem.at[k, t])
                pass_on(k)
        for k in range(stage * per, (stage + 1) * per):
            for o in others_t:
                arrived(seen.at[k, o], seen_sem.at[k, o])
        block = seen[stage * per : (stage + 1) * per]
        block = block.reshape(n_q * share, block.shape[3])
        width = 2 * head_dim
        for h in range(heads):
            at = slice(h * width, (h + 1) * width)
            product = jnp.dot(block, weights[:, at], preferred_element_type=jnp.float32)
            partial[stage, :, :, at] = product.reshape(n_q, share, width)
        for k, o in enumerate(others_q):
            send(
                partial.at[stage, o],
                landed.at[stage, k],
                sum_send.at[stage, k],
                sum_recv.at[stage, k],
                (s, o, t),
            )

    def finish(stage):
        for k in range(n_q - 1):
            arrived(landed.at[stage, k], sum_recv.at[stage, k])
        for h in range(heads):
            at_k = slice(2 * h * head_dim, (2 * h + 1) * head_dim)
            at_v = slice((2 * h + 1) * head_dim, (2 * h + 2) * head_dim)
            raw_k = partial[stage, q, :, at_k]
            raw_v = partial[stage, q, :, at_v]
            for k in range(n_q - 1):
                raw_k += landed[stage, k, :, at_k]
                raw_v += landed[stage, k, :, at_v]
            mean = jnp.mean(raw_k * raw_k, axis=-1, keepdims=True)
            scaled = raw_k * lax.rsqrt(mean + eps_norm) * gain[...]
            both = jnp.concatenate([scaled, raw_v], axis=0).astype(jnp.bfloat16)
            ready[stage, :, h * head_dim : (h + 1) * head_dim] = both
        for k, o in enumerate(others_q):
            send(
                ready.at[stage],
                gathered.at[stage, q],
                kv_send.at[stage, k],
                kv_recv.at[stage, q],
                (s, o, t),
            )
        gathered[stage, q] = ready[stage]

    def collect(stage):
        for o in others_q:
            arrived(gathered.at[stage, o], kv_recv.at[stage, o])
        block = gathered[stage].astype(jnp.float32)
        at = slice(stage * n_q * share, (stage + 1) * n_q * share)
        shape = (n_q * share, heads * head_dim)
        key_ref[at, :] = block[:, :share].reshape(shape).astype(jnp.bfloat16)
        value_ref[at, :] = block[:, share:].reshape(shape).astype(jnp.bfloat16)

    for stage in range(stages):
        project(stage)
        if stage >= 2:
            finish(stage - 2)
    for stage in range(max(stages - 2, 0), stages):
        finish(stage)
    for stage in range(stages):
        collect(stage)
    stage_queries.wait()
    for copy in sent:
        copy.wait_send()


def attend_kernel(head_dim, group, pair, q_ref, k_ref, v_ref, gate_ref, out_hbm, out_ref, out_sem):
    many = k_ref.shape[1] // head_dim
    rows = k_ref.shape[0]
    scale = head_dim ** (-0.5)

    def diagonal(block):
        if pair == 1:
            return block
        zero = jnp.zeros_like(block)
        return jnp.concatenate(
            [jnp.concatenate([block, zero], 1), jnp.concatenate([zero, block], 1)], 0
        )

    keys, values = [], []
    ones = diagonal(jnp.ones((rows, head_dim), jnp.bfloat16))
    for i in range(many):
        at = slice(i * head_dim, (i + 1) * head_dim)
        keys.append(diagonal(k_ref[:, at]))
        values.append(diagonal(v_ref[:, at]))
    wide = pair * head_dim
    units = range(0, many * group, pair)

    def score(g):
        return lax.dot_general(
            q_ref[0, :, g * head_dim : g * head_dim + wide],
            keys[g // group],
            (((1,), (1,)), ((), ())),
            preferred_element_type=jnp.float32,
        )

    def soften(scores):
        exps = []
        for p in range(pair):
            part = scores[:, p * rows : (p + 1) * rows]
            peak = jnp.max(part, axis=-1, keepdims=True)
            exps.append(jnp.exp((part - peak) * scale).astype(jnp.bfloat16))
        return exps[0] if pair == 1 else jnp.concatenate(exps, 1)

    copies = []

    def mix(exps, g):
        gates = [jnp.full((1, head_dim), gate_ref[0, g + p]) for p in range(pair)]
        gates = gates[0] if pair == 1 else jnp.concatenate(gates, 1)
        mixed = jnp.dot(exps, values[g // group], preferred_element_type=jnp.float32)
        total = jnp.dot(exps, ones, preferred_element_type=jnp.float32)
        result = mixed / total * jnp.tanh(gates)
        at = slice(g * head_dim, g * head_dim + wide)
        out_ref[0, :, at] = result.astype(jnp.bfloat16)
        copy = pltpu.make_async_copy(
            out_ref.at[:, :, at], out_hbm.at[:, :, at], out_sem.at[len(copies)]
        )
        copy.start()
        copies.append(copy)

    depth = 2
    waiting_scores, waiting_exps = [], []
    for step in range(len(units) + 2 * depth):
        if step < len(units):
            waiting_scores.append(score(units[step]))
        if depth <= step < len(units) + depth:
            waiting_exps.append(soften(waiting_scores.pop(0)))
        if step >= 2 * depth:
            mix(waiting_exps.pop(0), units[step - 2 * depth])
    for copy in copies:
        copy.wait()


def local(sizes, queries, vision, kv_weight, key_gain, head_gate):
    n_s, n_q, n_t = sizes
    head_dim = key_gain.shape[1]
    shard, features = vision.shape
    columns = kv_weight.shape[2]
    rows = shard * n_s * n_t
    stages = 1
    for tried in (2, 4):
        if n_s % tried == 0 and rows % (tried * 8 * n_q) == 0:
            stages = tried
    share = rows // (stages * n_q)
    hbm = pl.BlockSpec(memory_space=pltpu.HBM)
    vmem = pl.BlockSpec(memory_space=pltpu.VMEM)
    dma = pltpu.SemaphoreType.DMA
    keys, values, staged = pl.pallas_call(
        functools.partial(project_kernel, sizes, head_dim),
        out_shape=(
            pltpu.VMEM((rows, columns // 2), jnp.bfloat16),
            pltpu.VMEM((rows, columns // 2), jnp.bfloat16),
            pltpu.VMEM(queries.shape, jnp.bfloat16),
        ),
        in_specs=[hbm, hbm, hbm, hbm],
        out_specs=(vmem, vmem, vmem),
        scratch_shapes=[
            pltpu.VMEM((n_s, n_t, shard, features), jnp.bfloat16),
            pltpu.VMEM((features, columns), jnp.bfloat16),
            pltpu.VMEM(key_gain.shape, jnp.float32),
            pltpu.VMEM((stages, n_q, share, columns), jnp.float32),
            pltpu.VMEM((stages, n_q - 1, share, columns), jnp.float32),
            pltpu.VMEM((stages, 2 * share, columns // 2), jnp.bfloat16),
            pltpu.VMEM((stages, n_q, 2 * share, columns // 2), jnp.bfloat16),
            dma((4,)),
            dma((n_s - 1,)),
            dma((n_s, n_t - 1)),
            dma((n_s, n_t)),
            dma((stages, n_q - 1)),
            dma((stages, n_q - 1)),
            dma((stages, n_q - 1)),
            dma((stages, n_q)),
        ],
        compiler_params=pltpu.CompilerParams(
            collective_id=0, has_side_effects=True, vmem_limit_bytes=24 << 20
        ),
        name="project",
    )(*[pltpu.with_memory_space_constraint(x, pltpu.HBM) for x in (vision, kv_weight, key_gain, queries)])

    pair_heads = columns // (2 * head_dim)
    heads = head_gate.shape[1]
    group = heads // pair_heads
    pair = 2 if group % 2 == 0 and rows == head_dim else 1
    return pl.pallas_call(
        functools.partial(attend_kernel, head_dim, group, pair),
        out_shape=jax.ShapeDtypeStruct(queries.shape, jnp.bfloat16),
        in_specs=[vmem, vmem, vmem, pl.BlockSpec(memory_space=pltpu.SMEM)],
        out_specs=hbm,
        scratch_shapes=[pltpu.VMEM(queries.shape, jnp.bfloat16), dma((heads // pair,))],
        compiler_params=pltpu.CompilerParams(vmem_limit_bytes=24 << 20),
        name="attend",
    )(staged, keys, values, head_gate)


def solution(mesh):
    sizes = tuple(mesh.shape[name] for name in ("section", "seq", "tp"))
    return jax.shard_map(
        functools.partial(local, sizes),
        mesh=mesh,
        in_specs=(
            P("section", "seq", "tp"),
            P(("section", "tp"), "seq"),
            P("section", "seq", "tp"),
            P("section", None),
            P("section", "tp"),
        ),
        out_specs=P("section", "seq", "tp"),
        check_vma=False,
    )
```

```python
import functools
import math

import jax
import jax.numpy as jnp
from jax import lax
from jax.experimental import pallas as pl
from jax.experimental.pallas import tpu as pltpu
from jax.sharding import PartitionSpec as P

MESH = pl.DeviceIdType.MESH
eps_norm = 1e-05


def project_kernel(
    sizes,
    plan,
    vision_ref,
    weight_ref,
    gain_ref,
    query_ref,
    kv_ref,
    staged_ref,
    seen,
    weights,
    gain,
    partial,
    landed,
    ready,
    load_sem,
    far_send,
    chip_send,
    pass_send,
    seen_sem,
    sum_send,
    sum_recv,
    kv_send,
    kv_recv,
    in_s,
    in_q,
    in_t,
):
    n_s, n_q, n_t = sizes
    s, q, t = lax.axis_index("section"), lax.axis_index("seq"), lax.axis_index("tp")
    inner, head_dim = kv_ref.shape[0], kv_ref.shape[3]
    stages = len(plan)
    shard = seen.shape[2]
    groups = math.gcd(inner, n_q)
    each = inner // groups
    blocks = n_q // groups
    part = n_t * shard // blocks
    width = each * 2 * head_dim
    half = n_s // 2 if n_s % 2 == 0 else n_s
    last = n_t - 1

    def section_of(k):
        base = (s // half) * half
        return lax.rem(base + (k // half) * half, n_s) + lax.rem(s + k, half)

    def partner(i, k):
        if groups & (groups - 1):
            return lax.rem(i + k, groups)
        result, bit = i, 1
        while bit < groups:
            if k & bit:
                result = result + bit - 2 * bit * ((i // bit) % 2)
            bit *= 2
        return result

    def at_device(peer):
        return tuple(0 * s + c if isinstance(c, int) else c for c in peer)

    def signal(sem, peer):
        pl.semaphore_signal(sem, inc=1, device_id=at_device(peer), device_id_type=MESH)

    own = pltpu.make_async_copy(vision_ref, seen.at[s, t], load_sem.at[0])
    load = pltpu.make_async_copy(weight_ref.at[0], weights, load_sem.at[1])
    load_gain = pltpu.make_async_copy(gain_ref, gain, load_sem.at[2])
    stage_queries = pltpu.make_async_copy(query_ref, staged_ref, load_sem.at[3])

    barrier = pltpu.get_barrier_semaphore()
    for o in range(1, n_s):
        for p in range(n_t):
            @pl.when((o > s) & ((t == 0) | (p == 0)))
            def _():
                signal(barrier, (o, q, p))
    for o in range(1, n_q):
        for p in range(n_t):
            @pl.when((o > q) & ((t == last) | (p == last)))
            def _():
                signal(barrier, (s, o, p))
    for p in range(1, n_t):
        @pl.when(p > t)
        def _():
            signal(barrier, (s, q, p))
    own.start()
    load.start()
    load_gain.start()
    stage_queries.start()
    earlier = s * jnp.where(t == 0, n_t, 1) + q * jnp.where(t == last, n_t, 1) + t

    @pl.when(earlier > 0)
    def _():
        pl.semaphore_wait(barrier, earlier)

    sent = []

    def start(build, when=None):
        def make():
            src, dst, send_sem, recv_sem, peer = build()
            return pltpu.make_async_remote_copy(
                src_ref=src,
                dst_ref=dst,
                send_sem=send_sem,
                recv_sem=recv_sem,
                device_id=at_device(peer),
                device_id_type=MESH,
            )

        if when is None:
            make().start()
        else:
            @pl.when(when)
            def _():
                make().start()
        sent.append((make, when))

    def send(src, dst, send_sem, recv_sem, peer, when=None):
        start(lambda: (src, dst, send_sem, recv_sem, peer), when)

    def arrived(dst, sem):
        pltpu.make_async_copy(dst, dst, sem).wait()

    def far(o, when):
        send(seen.at[s, t], seen.at[s, t], far_send.at[o], seen_sem.at[s, t], (o, q, 0), when)

    own.wait()
    for o in range(n_s - 1):
        far(o, o < s)
    for o in range(n_s - 1):
        for p in range(n_t):
            @pl.when((o < s) & (t == 0))
            def _():
                signal(in_s.at[s], (o, q, p))
    for p in range(n_t - 1):
        @pl.when(p < t)
        def _():
            signal(in_t.at[t], (s, q, p))
    for o in range(n_q - 1):
        for p in range(n_t):
            @pl.when((o < q) & ((t == last) | (p == last)))
            def _():
                signal(in_q.at[q, t], (s, o, p))
    for p in range(n_t):
        @pl.when(p > t)
        def _():
            pl.semaphore_wait(in_t.at[p], 1)
        send(seen.at[s, t], seen.at[s, t], chip_send.at[p], seen_sem.at[s, t], (s, q, p), p != t)

    def upward():
        for o in range(1, n_s):
            @pl.when(o > s)
            def _():
                pl.semaphore_wait(in_s.at[o], 1)
            far(o, o > s)

    def project(stage):
        for k in plan[stage]:
            if k > 0:
                sec = section_of(k)
                for p in range(n_t):
                    arrived(seen.at[sec, p], seen_sem.at[sec, p])
                    for o in range(1, n_t):
                        send(
                            seen.at[sec, p],
                            seen.at[sec, p],
                            pass_send.at[k, p, o],
                            seen_sem.at[sec, p],
                            (s, q, o),
                            t == 0,
                        )
            else:
                for p in range(n_t):
                    @pl.when(p != t)
                    def _():
                        arrived(seen.at[s, p], seen_sem.at[s, p])
        if stage == 0:
            load.wait()
        parts = [
            seen[section_of(k) if k else s].reshape(n_t * shard, seen.shape[3])
            for k in plan[stage]
        ]
        share = len(parts) * part
        first = plan[stage][0] * part
        rows_at = pl.ds(first, share)
        block = parts[0] if len(parts) == 1 else jnp.concatenate(parts, 0)
        for k in range(groups - 1, -1, -1):
            g = partner(lax.rem(q, groups), k)
            at = pl.ds(pl.multiple_of(g * width, width), width)
            product = jnp.dot(block, weights[:, at], preferred_element_type=jnp.float32)
            for b in range(blocks):
                o = b * groups + g
                partial[o, rows_at] = product[b * share : (b + 1) * share]
                if stage == 0:
                    @pl.when(o > q)
                    def _():
                        pl.semaphore_wait(in_q.at[o, last], 1)
                send(
                    partial.at[o, rows_at],
                    landed.at[t, q, rows_at],
                    sum_send.at[stage, o],
                    sum_recv.at[stage, t, q],
                    (s, o, last),
                    (o != q) | (t != last),
                )

    def place(stage, o):
        share = len(plan[stage]) * part
        row = plan[stage][0] * n_t * shard + (o // groups) * share
        if not isinstance(o, int):
            row = pl.multiple_of(row, share)
        return pl.ds(o % groups * each, each), pl.ds(row, share)

    others = [partner(q, k) if groups == n_q else lax.rem(q + k, n_q) for k in range(n_q)]
    mine_at = [place(stage, q) for stage in range(stages)]

    def finish(stage):
        own_at = pl.ds(plan[stage][0] * part, len(plan[stage]) * part)
        for p in range(n_t):
            for k in range(n_q):
                o = lax.rem(q + k, n_q)
                if p != last or k > 0:
                    arrived(landed.at[p, o, own_at], sum_recv.at[stage, p, o])
            for h in range(each):
                at_k = slice(2 * h * head_dim, (2 * h + 1) * head_dim)
                at_v = slice((2 * h + 1) * head_dim, (2 * h + 2) * head_dim)
                mine = partial.at[q] if p == last else landed.at[p, q]
                raw_k, raw_v = mine[own_at, at_k], mine[own_at, at_v]
                for k in range(1, n_q):
                    o = lax.rem(q + k, n_q)
                    raw_k += landed[p, o, own_at, at_k]
                    raw_v += landed[p, o, own_at, at_v]
                mean = jnp.mean(raw_k * raw_k, axis=-1, keepdims=True)
                scaled = raw_k * lax.rsqrt(mean + eps_norm) * gain[...]
                ready[p, h, 0, own_at] = scaled.astype(jnp.bfloat16)
                ready[p, h, 1, own_at] = raw_v.astype(jnp.bfloat16)
            heads_at, rows_at = mine_at[stage]
            for k in range(n_q - 1, -1, -1):
                if k == 0 and p == last:
                    kv_ref[heads_at, :, rows_at, :] = ready[p, :, :, own_at]
                    continue
                o = others[k]
                if stage == 0 and p != last and k > 0:
                    @pl.when(o > q)
                    def _():
                        pl.semaphore_wait(in_q.at[o, p], 1)
                start(
                    lambda p=p, o=o: (
                        ready.at[p, :, :, own_at],
                        kv_ref.at[heads_at, :, rows_at, :],
                        kv_send.at[stage, p, o],
                        kv_recv.at[stage, q],
                        (s, o, p),
                    )
                )

    def owner(step):
        before = len(sent)

        @pl.when(t == last)
        def _():
            step()
        sent[before:] = [(make, t == last) for make, _ in sent[before:]]

    def collect(stage):
        for o in range(n_q):
            heads_at, rows_at = place(stage, o)

            @pl.when((o != q) | (t != last))
            def _():
                arrived(kv_ref.at[heads_at, :, rows_at, :], kv_recv.at[stage, o])

    load_gain.wait()
    upward()
    for stage in range(stages):
        project(stage)
        if stage >= 2:
            owner(functools.partial(finish, stage - 2))
    for stage in range(max(stages - 2, 0), stages):
        owner(functools.partial(finish, stage))
    for stage in range(stages):
        collect(stage)
    stage_queries.wait()
    for make, when in sent:
        if when is None:
            make().wait_send()
        else:
            @pl.when(when)
            def _():
                make().wait_send()


def attend_kernel(group, pair, q_ref, kv_ref, gate_ref, out_hbm, out_ref, out_sem):
    many, _, rows, head_dim = kv_ref.shape
    scale = head_dim ** (-0.5)

    def diagonal(block):
        if pair == 1:
            return block
        zero = jnp.zeros_like(block)
        return jnp.concatenate(
            [jnp.concatenate([block, zero], 1), jnp.concatenate([zero, block], 1)], 0
        )

    keys, values = [], []
    ones = diagonal(jnp.ones((rows, head_dim), jnp.bfloat16))
    for i in range(many):
        keys.append(diagonal(kv_ref[i, 0]))
        values.append(diagonal(kv_ref[i, 1]))
    wide = pair * head_dim
    units = range(0, many * group, pair)

    def score(g):
        return lax.dot_general(
            q_ref[0, :, g * head_dim : g * head_dim + wide],
            keys[g // group],
            (((1,), (1,)), ((), ())),
            preferred_element_type=jnp.float32,
        )

    def soften(scores):
        exps = []
        for p in range(pair):
            part = scores[:, p * rows : (p + 1) * rows]
            peak = jnp.max(part, axis=-1, keepdims=True)
            exps.append(jnp.exp((part - peak) * scale).astype(jnp.bfloat16))
        return exps[0] if pair == 1 else jnp.concatenate(exps, 1)

    copies = []

    def mix(exps, g):
        gates = [jnp.full((1, head_dim), gate_ref[0, g + p]) for p in range(pair)]
        gates = gates[0] if pair == 1 else jnp.concatenate(gates, 1)
        mixed = jnp.dot(exps, values[g // group], preferred_element_type=jnp.float32)
        total = jnp.dot(exps, ones, preferred_element_type=jnp.float32)
        result = mixed / total * jnp.tanh(gates)
        at = slice(g * head_dim, g * head_dim + wide)
        out_ref[0, :, at] = result.astype(jnp.bfloat16)
        copy = pltpu.make_async_copy(
            out_ref.at[:, :, at], out_hbm.at[:, :, at], out_sem.at[len(copies)]
        )
        copy.start()
        copies.append(copy)

    depth = 2
    waiting_scores, waiting_exps = [], []
    for step in range(len(units) + 2 * depth):
        if step < len(units):
            waiting_scores.append(score(units[step]))
        if depth <= step < len(units) + depth:
            waiting_exps.append(soften(waiting_scores.pop(0)))
        if step >= 2 * depth:
            mix(waiting_exps.pop(0), units[step - 2 * depth])
    for copy in copies:
        copy.wait()


def local(sizes, queries, vision, kv_weight, key_gain, head_gate):
    n_s, n_q, n_t = sizes
    head_dim = key_gain.shape[1]
    shard, features = vision.shape
    columns = kv_weight.shape[2]
    rows = shard * n_s * n_t
    inner = columns // (2 * head_dim)
    blocks = n_q // math.gcd(inner, n_q)
    step = max(n_s // 4, 1)
    while step < n_s and step * n_t * shard % (16 * blocks):
        step += 1
    cuts = [k for k in (0, step, 2 * step) if k < n_s] + [n_s]
    plan = [list(range(a, b)) for a, b in zip(cuts, cuts[1:])]
    stages = len(plan)
    each = inner // math.gcd(inner, n_q)
    hbm = pl.BlockSpec(memory_space=pltpu.HBM)
    vmem = pl.BlockSpec(memory_space=pltpu.VMEM)
    dma = pltpu.SemaphoreType.DMA
    regular = pltpu.SemaphoreType.REGULAR
    kv, staged = pl.pallas_call(
        functools.partial(project_kernel, sizes, plan),
        out_shape=(
            pltpu.VMEM((inner, 2, rows, head_dim), jnp.bfloat16),
            pltpu.VMEM(queries.shape, jnp.bfloat16),
        ),
        in_specs=[hbm, hbm, hbm, hbm],
        out_specs=(vmem, vmem),
        scratch_shapes=[
            pltpu.VMEM((n_s, n_t, shard, features), jnp.bfloat16),
            pltpu.VMEM((features, columns), jnp.bfloat16),
            pltpu.VMEM(key_gain.shape, jnp.float32),
            pltpu.VMEM((n_q, rows // blocks, each * 2 * head_dim), jnp.float32),
            pltpu.VMEM((n_t, n_q, rows // blocks, each * 2 * head_dim), jnp.float32),
            pltpu.VMEM((n_t, each, 2, rows // blocks, head_dim), jnp.bfloat16),
            dma((4,)),
            dma((n_s,)),
            dma((n_t,)),
            dma((n_s, n_t, n_t)),
            dma((n_s, n_t)),
            dma((stages, n_q)),
            dma((stages, n_t, n_q)),
            dma((stages, n_t, n_q)),
            dma((stages, n_q)),
            regular((n_s,)),
            regular((n_q, n_t)),
            regular((n_t,)),
        ],
        compiler_params=pltpu.CompilerParams(
            collective_id=0, has_side_effects=True, vmem_limit_bytes=24 << 20
        ),
        name="project",
    )(*[pltpu.with_memory_space_constraint(x, pltpu.HBM) for x in (vision, kv_weight, key_gain, queries)])

    heads = head_gate.shape[1]
    group = heads // inner
    pair = 2 if group % 2 == 0 and rows == head_dim else 1
    return pl.pallas_call(
        functools.partial(attend_kernel, group, pair),
        out_shape=jax.ShapeDtypeStruct(queries.shape, jnp.bfloat16),
        in_specs=[vmem, vmem, pl.BlockSpec(memory_space=pltpu.SMEM)],
        out_specs=hbm,
        scratch_shapes=[pltpu.VMEM(queries.shape, jnp.bfloat16), dma((heads // pair,))],
        compiler_params=pltpu.CompilerParams(vmem_limit_bytes=24 << 20),
        name="attend",
    )(staged, kv, head_gate)


def solution(mesh):
    sizes = tuple(mesh.shape[name] for name in ("section", "seq", "tp"))
    return jax.shard_map(
        functools.partial(local, sizes),
        mesh=mesh,
        in_specs=(
            P("section", "seq", "tp"),
            P(("section", "tp"), "seq"),
            P("section", "seq", "tp"),
            P("section", None),
            P("section", "tp"),
        ),
        out_specs=P("section", "seq", "tp"),
        check_vma=False,
    )
```

```python
import functools
import math

import jax
import jax.numpy as jnp
from jax import lax
from jax.experimental import pallas as pl
from jax.experimental.pallas import tpu as pltpu
from jax.sharding import PartitionSpec as P

MESH = pl.DeviceIdType.MESH
eps_norm = 1e-05


def partner(i, k, n):
    if n & (n - 1):
        return lax.rem(i + k, n)
    result, bit = i, 1
    while bit < n:
        if k & bit:
            result = result + bit - 2 * bit * ((i // bit) % 2)
        bit *= 2
    return result


def attention(group, pair, q_ref, kv_ref, gate_ref, heads, done):
    _, _, rows, head_dim = kv_ref.shape
    scale = head_dim ** (-0.5)

    def diagonal(block):
        if pair == 1:
            return block
        zero = jnp.zeros_like(block)
        return jnp.concatenate(
            [jnp.concatenate([block, zero], 1), jnp.concatenate([zero, block], 1)], 0
        )

    ones = diagonal(jnp.ones((rows, head_dim), jnp.bfloat16))
    keys = [diagonal(kv_ref[h, 0]) for h in heads]
    values = [diagonal(kv_ref[h, 1]) for h in heads]
    wide = pair * head_dim
    units = [(i, g) for i in range(len(heads)) for g in range(0, group, pair)]

    def score(i, g):
        start = pl.multiple_of(heads[i] * (group * head_dim) + g * head_dim, wide)
        return lax.dot_general(
            q_ref[0, :, pl.ds(start, wide)],
            keys[i],
            (((1,), (1,)), ((), ())),
            preferred_element_type=jnp.float32,
        )

    def soften(scores):
        exps = []
        for p in range(pair):
            part = scores[:, p * rows : (p + 1) * rows]
            peak = jnp.max(part, axis=-1, keepdims=True)
            exps.append(jnp.exp((part - peak) * scale).astype(jnp.bfloat16))
        return exps[0] if pair == 1 else jnp.concatenate(exps, 1)

    def mix(exps, i, g):
        gates = [
            jnp.full((1, head_dim), gate_ref[0, heads[i] * group + g + p]) for p in range(pair)
        ]
        gates = gates[0] if pair == 1 else jnp.concatenate(gates, 1)
        mixed = jnp.dot(exps, values[i], preferred_element_type=jnp.float32)
        total = jnp.dot(exps, ones, preferred_element_type=jnp.float32)
        result = mixed / total * jnp.tanh(gates)
        done(i, g, result.astype(jnp.bfloat16))

    depth = 2
    waiting_scores, waiting_exps = [], []
    for step in range(len(units) + 2 * depth):
        if step < len(units):
            waiting_scores.append(score(*units[step]))
        if depth <= step < len(units) + depth:
            waiting_exps.append(soften(waiting_scores.pop(0)))
        if step >= 2 * depth:
            mix(waiting_exps.pop(0), *units[step - 2 * depth])


def attend_kernel(
    group, pair, early, late, q_ref, kv_ref, gate_ref, *rest
):
    early_ref = rest[0] if early else None
    out_hbm, out_ref, out_sem = rest[-3:]
    head_dim = kv_ref.shape[3]
    groups = len(early) + len(late)
    each = kv_ref.shape[0] // groups
    me = lax.rem(lax.axis_index("seq"), groups)
    copies = []

    def write(src, head, g, wide):
        start = pl.multiple_of(head * (group * head_dim) + g * head_dim, wide)
        copy = pltpu.make_async_copy(
            src, out_hbm.at[:, :, pl.ds(start, wide)], out_sem.at[len(copies)]
        )
        copy.start()
        copies.append(copy)

    block = each * group * head_dim
    for j, k in enumerate(early):
        write(early_ref.at[:, :, j * block : (j + 1) * block], partner(me, k, groups) * each, 0, block)
    heads = [partner(me, k, groups) * each + i for k in late for i in range(each)]
    wide = pair * head_dim

    def done(i, g, result):
        at = slice((i * group + g) * head_dim, (i * group + g) * head_dim + wide)
        out_ref[0, :, at] = result
        write(out_ref.at[:, :, at], heads[i], g, wide)

    attention(group, pair, q_ref, kv_ref, gate_ref, heads, done)
    for copy in copies:
        copy.wait()


def project_kernel(
    sizes,
    plan,
    group,
    pair,
    early,
    vision_ref,
    weight_ref,
    gain_ref,
    query_ref,
    gate_ref,
    kv_ref,
    staged_ref,
    *rest,
):
    early_ref = rest[0] if early else None
    scratch = rest[1:] if early else rest
    return project_steps(
        sizes, plan, group, pair, early, vision_ref, weight_ref, gain_ref, query_ref, gate_ref,
        kv_ref, staged_ref, early_ref, *scratch
    )


def project_steps(
    sizes,
    plan,
    group,
    pair,
    early,
    vision_ref,
    weight_ref,
    gain_ref,
    query_ref,
    gate_ref,
    kv_ref,
    staged_ref,
    early_ref,
    seen,
    weights,
    gain,
    partial,
    landed,
    ready,
    gate,
    load_sem,
    far_send,
    chip_send,
    pass_send,
    seen_sem,
    sum_send,
    sum_recv,
    kv_send,
    kv_recv,
    in_s,
    in_q,
    in_t,
):
    n_s, n_q, n_t = sizes
    s, q, t = lax.axis_index("section"), lax.axis_index("seq"), lax.axis_index("tp")
    inner, head_dim = kv_ref.shape[0], kv_ref.shape[3]
    stages = len(plan)
    shard = seen.shape[2]
    groups = math.gcd(inner, n_q)
    each = inner // groups
    blocks = n_q // groups
    part = n_t * shard // blocks
    width = each * 2 * head_dim
    half = n_s // 2 if n_s % 2 == 0 else n_s
    last = n_t - 1

    def section_of(k):
        base = (s // half) * half
        return lax.rem(base + (k // half) * half, n_s) + lax.rem(s + k, half)

    def at_device(peer):
        return tuple(0 * s + c if isinstance(c, int) else c for c in peer)

    def signal(sem, peer):
        pl.semaphore_signal(sem, inc=1, device_id=at_device(peer), device_id_type=MESH)

    own = pltpu.make_async_copy(vision_ref, seen.at[s, t], load_sem.at[0])
    load = pltpu.make_async_copy(weight_ref.at[0], weights, load_sem.at[1])
    load_gain = pltpu.make_async_copy(gain_ref, gain, load_sem.at[2])
    stage_queries = pltpu.make_async_copy(query_ref, staged_ref, load_sem.at[3])
    load_gate = pltpu.make_async_copy(gate_ref, gate, load_sem.at[4])

    barrier = pltpu.get_barrier_semaphore()
    for o in range(1, n_s):
        for p in range(n_t):
            @pl.when((o > s) & ((t == 0) | (p == 0)))
            def _():
                signal(barrier, (o, q, p))
    for o in range(1, n_q):
        for p in range(n_t):
            @pl.when((o > q) & ((t == last) | (p == last)))
            def _():
                signal(barrier, (s, o, p))
    for p in range(1, n_t):
        @pl.when(p > t)
        def _():
            signal(barrier, (s, q, p))
    own.start()
    load.start()
    load_gain.start()
    load_gate.start()
    stage_queries.start()
    earlier = s * jnp.where(t == 0, n_t, 1) + q * jnp.where(t == last, n_t, 1) + t

    @pl.when(earlier > 0)
    def _():
        pl.semaphore_wait(barrier, earlier)

    sent = []

    def start(build, when=None):
        def make():
            src, dst, send_sem, recv_sem, peer = build()
            return pltpu.make_async_remote_copy(
                src_ref=src,
                dst_ref=dst,
                send_sem=send_sem,
                recv_sem=recv_sem,
                device_id=at_device(peer),
                device_id_type=MESH,
            )

        if when is None:
            make().start()
        else:
            @pl.when(when)
            def _():
                make().start()
        sent.append((make, when))

    def send(src, dst, send_sem, recv_sem, peer, when=None):
        start(lambda: (src, dst, send_sem, recv_sem, peer), when)

    def arrived(dst, sem):
        pltpu.make_async_copy(dst, dst, sem).wait()

    def far(o, when):
        send(seen.at[s, t], seen.at[s, t], far_send.at[o], seen_sem.at[s, t], (o, q, 0), when)

    own.wait()
    for o in range(n_s - 1):
        for p in range(n_t):
            @pl.when((o < s) & (t == 0))
            def _():
                signal(in_s.at[s], (o, q, p))
    for p in range(n_t - 1):
        @pl.when(p < t)
        def _():
            signal(in_t.at[t], (s, q, p))
    for o in range(n_q - 1):
        for p in range(n_t):
            @pl.when((o < q) & ((t == last) | (p == last)))
            def _():
                signal(in_q.at[q, t], (s, o, p))
    for o in range(n_s - 2):
        far(o, (o < s) & (s < n_s - 1))
    far(n_s - 2, s == n_s - 1)
    for p in range(n_t):
        @pl.when(p > t)
        def _():
            pl.semaphore_wait(in_t.at[p], 1)
        send(seen.at[s, t], seen.at[s, t], chip_send.at[p], seen_sem.at[s, t], (s, q, p), p != t)
    @pl.when(s == n_s - 1)
    def _():
        for p in range(n_t):
            @pl.when(p != t)
            def _():
                arrived(seen.at[s, p], seen_sem.at[s, p])
    if n_s > 2:
        far(0, s == n_s - 1)

    def upward():
        for o in range(1, n_s):
            @pl.when(o > s)
            def _():
                pl.semaphore_wait(in_s.at[o], 1)
            far(o, o > s)

    def project(stage):
        for k in plan[stage]:
            if k > 0:
                sec = section_of(k)
                for p in range(n_t):
                    arrived(seen.at[sec, p], seen_sem.at[sec, p])
                    for o in range(1, n_t):
                        send(
                            seen.at[sec, p],
                            seen.at[sec, p],
                            pass_send.at[k, p, o],
                            seen_sem.at[sec, p],
                            (s, q, o),
                            t == 0,
                        )
            else:
                for p in range(n_t):
                    @pl.when((p != t) & (s < n_s - 1))
                    def _():
                        arrived(seen.at[s, p], seen_sem.at[s, p])
        if stage == 0:
            load.wait()
        parts = [
            seen[section_of(k) if k else s].reshape(n_t * shard, seen.shape[3])
            for k in plan[stage]
        ]
        share = len(parts) * part
        first = plan[stage][0] * part
        rows_at = pl.ds(first, share)
        block = parts[0] if len(parts) == 1 else jnp.concatenate(parts, 0)
        for k in range(groups - 1, -1, -1):
            g = partner(lax.rem(q, groups), k, groups)
            at = pl.ds(pl.multiple_of(g * width, width), width)
            product = jnp.dot(block, weights[:, at], preferred_element_type=jnp.float32)
            for b in range(blocks):
                o = b * groups + g
                partial[o, rows_at] = product[b * share : (b + 1) * share]
                if stage == 0:
                    @pl.when(o > q)
                    def _():
                        pl.semaphore_wait(in_q.at[o, last], 1)
                send(
                    partial.at[o, rows_at],
                    landed.at[t, q, rows_at],
                    sum_send.at[stage, o],
                    sum_recv.at[stage, t, q],
                    (s, o, last),
                    (o != q) | (t != last),
                )

    def place(stage, o):
        share = len(plan[stage]) * part
        row = plan[stage][0] * n_t * shard + (o // groups) * share
        if not isinstance(o, int):
            row = pl.multiple_of(row, share)
        return pl.ds(o % groups * each, each), pl.ds(row, share)

    others = [partner(q, k, n_q) if groups == n_q else lax.rem(q + k, n_q) for k in range(n_q)]
    mine_at = [place(stage, q) for stage in range(stages)]

    def finish(stage):
        own_at = pl.ds(plan[stage][0] * part, len(plan[stage]) * part)
        for p in range(n_t):
            for k in range(n_q):
                o = lax.rem(q + k, n_q)
                if p != last or k > 0:
                    arrived(landed.at[p, o, own_at], sum_recv.at[stage, p, o])
            for h in range(each):
                at_k = slice(2 * h * head_dim, (2 * h + 1) * head_dim)
                at_v = slice((2 * h + 1) * head_dim, (2 * h + 2) * head_dim)
                mine = partial.at[q] if p == last else landed.at[p, q]
                raw_k, raw_v = mine[own_at, at_k], mine[own_at, at_v]
                for k in range(1, n_q):
                    o = lax.rem(q + k, n_q)
                    raw_k += landed[p, o, own_at, at_k]
                    raw_v += landed[p, o, own_at, at_v]
                mean = jnp.mean(raw_k * raw_k, axis=-1, keepdims=True)
                scaled = raw_k * lax.rsqrt(mean + eps_norm) * gain[...]
                ready[p, h, 0, own_at] = scaled.astype(jnp.bfloat16)
                ready[p, h, 1, own_at] = raw_v.astype(jnp.bfloat16)
            heads_at, rows_at = mine_at[stage]
            for k in range(n_q - 1, -1, -1):
                if k == 0 and p == last:
                    kv_ref[heads_at, :, rows_at, :] = ready[p, :, :, own_at]
                    continue
                o = others[k]
                if stage == 0 and p != last and k > 0:
                    @pl.when(o > q)
                    def _():
                        pl.semaphore_wait(in_q.at[o, p], 1)
                start(
                    lambda p=p, o=o: (
                        ready.at[p, :, :, own_at],
                        kv_ref.at[heads_at, :, rows_at, :],
                        kv_send.at[stage, p, o],
                        kv_recv.at[stage, q],
                        (s, o, p),
                    )
                )

    def owner(step):
        before = len(sent)

        @pl.when(t == last)
        def _():
            step()
        sent[before:] = [(make, t == last) for make, _ in sent[before:]]

    def collect(stage, o):
        heads_at, rows_at = place(stage, o)

        @pl.when((o != q) | (t != last))
        def _():
            arrived(kv_ref.at[heads_at, :, rows_at, :], kv_recv.at[stage, o])

    def attend_early(j):
        def done(i, g, result):
            at = ((j * each + i) * group + g) * head_dim
            early_ref[0, :, at : at + pair * head_dim] = result

        first_head = partner(lax.rem(q, groups), early[j], groups) * each
        heads = [first_head + i for i in range(each)]
        attention(group, pair, staged_ref, kv_ref, gate, heads, done)

    load_gain.wait()
    upward()
    for stage in range(stages):
        project(stage)
        if stage == 0:
            for o in range(1, n_s - 2):
                far(o, s == n_s - 1)
        if stage >= 2:
            owner(functools.partial(finish, stage - 2))
    for stage in range(max(stages - 2, 0), stages):
        owner(functools.partial(finish, stage))
    stage_queries.wait()
    load_gate.wait()
    for j in range(len(early)):
        for stage in range(stages):
            collect(stage, others[early[j]])
        attend_early(j)
    for k in range(n_q):
        if k not in early:
            for stage in range(stages):
                collect(stage, others[k])
    for make, when in sent:
        if when is None:
            make().wait_send()
        else:
            @pl.when(when)
            def _():
                make().wait_send()


def local(sizes, queries, vision, kv_weight, key_gain, head_gate):
    n_s, n_q, n_t = sizes
    head_dim = key_gain.shape[1]
    shard, features = vision.shape
    columns = kv_weight.shape[2]
    rows = shard * n_s * n_t
    inner = columns // (2 * head_dim)
    blocks = n_q // math.gcd(inner, n_q)
    step = max(n_s // 4, 1)
    while step < n_s and step * n_t * shard % (16 * blocks):
        step += 1
    cuts = [k for k in (0, step, 2 * step) if k < n_s] + [n_s]
    plan = [list(range(a, b)) for a, b in zip(cuts, cuts[1:])]
    stages = len(plan)
    each = inner // math.gcd(inner, n_q)
    hbm = pl.BlockSpec(memory_space=pltpu.HBM)
    vmem = pl.BlockSpec(memory_space=pltpu.VMEM)
    dma = pltpu.SemaphoreType.DMA
    regular = pltpu.SemaphoreType.REGULAR
    heads = head_gate.shape[1]
    group = heads // inner
    pair = 2 if group % 2 == 0 and rows == head_dim else 1
    groups = n_q // blocks
    early = (0,) if blocks == 1 else ()
    late = tuple(k for k in range(groups) if k not in early)
    ahead = [pltpu.VMEM(queries.shape[:2] + (len(early) * each * group * head_dim,), jnp.bfloat16)]
    ahead = ahead if early else []
    smem = pl.BlockSpec(memory_space=pltpu.SMEM)
    kv, staged, *ahead = pl.pallas_call(
        functools.partial(project_kernel, sizes, plan, group, pair, early),
        out_shape=(
            pltpu.VMEM((inner, 2, rows, head_dim), jnp.bfloat16),
            pltpu.VMEM(queries.shape, jnp.bfloat16),
            *ahead,
        ),
        in_specs=[hbm] * 5,
        out_specs=(vmem, vmem) + (vmem,) * len(ahead),
        scratch_shapes=[
            pltpu.VMEM((n_s, n_t, shard, features), jnp.bfloat16),
            pltpu.VMEM((features, columns), jnp.bfloat16),
            pltpu.VMEM(key_gain.shape, jnp.float32),
            pltpu.VMEM((n_q, rows // blocks, each * 2 * head_dim), jnp.float32),
            pltpu.VMEM((n_t, n_q, rows // blocks, each * 2 * head_dim), jnp.float32),
            pltpu.VMEM((n_t, each, 2, rows // blocks, head_dim), jnp.bfloat16),
            pltpu.SMEM(head_gate.shape, jnp.float32),
            dma((5,)),
            dma((n_s,)),
            dma((n_t,)),
            dma((n_s, n_t, n_t)),
            dma((n_s, n_t)),
            dma((stages, n_q)),
            dma((stages, n_t, n_q)),
            dma((stages, n_t, n_q)),
            dma((stages, n_q)),
            regular((n_s,)),
            regular((n_q, n_t)),
            regular((n_t,)),
        ],
        compiler_params=pltpu.CompilerParams(
            collective_id=0, has_side_effects=True, vmem_limit_bytes=24 << 20
        ),
        name="project",
    )(
        *[
            pltpu.with_memory_space_constraint(x, pltpu.HBM)
            for x in (vision, kv_weight, key_gain, queries, head_gate)
        ]
    )

    return pl.pallas_call(
        functools.partial(attend_kernel, group, pair, early, late),
        out_shape=jax.ShapeDtypeStruct(queries.shape, jnp.bfloat16),
        in_specs=[vmem, vmem, smem] + [vmem] * len(ahead),
        out_specs=hbm,
        scratch_shapes=[
            pltpu.VMEM(queries.shape[:2] + (len(late) * each * group * head_dim,), jnp.bfloat16),
            dma((len(early) + len(late) * each * group // pair,)),
        ],
        compiler_params=pltpu.CompilerParams(vmem_limit_bytes=24 << 20),
        name="attend",
    )(staged, kv, head_gate, *ahead)


def solution(mesh):
    sizes = tuple(mesh.shape[name] for name in ("section", "seq", "tp"))
    return jax.shard_map(
        functools.partial(local, sizes),
        mesh=mesh,
        in_specs=(
            P("section", "seq", "tp"),
            P(("section", "tp"), "seq"),
            P("section", "seq", "tp"),
            P("section", None),
            P("section", "tp"),
        ),
        out_specs=P("section", "seq", "tp"),
        check_vma=False,
    )
```

```python
import functools
import math

import jax
import jax.numpy as jnp
from jax import lax
from jax.experimental import pallas as pl
from jax.experimental.pallas import tpu as pltpu
from jax.sharding import PartitionSpec as P

MESH = pl.DeviceIdType.MESH
eps_norm = 1e-05


def partner(i, k, n):
    if n & (n - 1):
        return lax.rem(i + k, n)
    result, bit = i, 1
    while bit < n:
        if k & bit:
            result = result + bit - 2 * bit * ((i // bit) % 2)
        bit *= 2
    return result


def attention(group, pair, q_ref, kv_ref, gate_ref, heads, done):
    _, _, rows, head_dim = kv_ref.shape
    scale = head_dim ** (-0.5)

    def diagonal(block):
        if pair == 1:
            return block
        zero = jnp.zeros_like(block)
        return jnp.concatenate(
            [jnp.concatenate([block, zero], 1), jnp.concatenate([zero, block], 1)], 0
        )

    ones = diagonal(jnp.ones((rows, head_dim), jnp.bfloat16))
    made = {}

    def block(i, kind):
        if (i, kind) not in made:
            made[i, kind] = diagonal(kv_ref[heads[i], kind])
        return made[i, kind]

    wide = pair * head_dim
    units = [(i, g) for i in range(len(heads)) for g in range(0, group, pair)]

    def score(i, g):
        start = pl.multiple_of(heads[i] * (group * head_dim) + g * head_dim, wide)
        return lax.dot_general(
            q_ref[0, :, pl.ds(start, wide)],
            block(i, 0),
            (((1,), (1,)), ((), ())),
            preferred_element_type=jnp.float32,
        )

    def soften(scores):
        exps = []
        for p in range(pair):
            part = scores[:, p * rows : (p + 1) * rows]
            peak = jnp.max(part, axis=-1, keepdims=True)
            exps.append(jnp.exp((part - peak) * scale).astype(jnp.bfloat16))
        return exps[0] if pair == 1 else jnp.concatenate(exps, 1)

    def mix(exps, i, g):
        gates = [
            jnp.full((1, head_dim), gate_ref[0, heads[i] * group + g + p]) for p in range(pair)
        ]
        gates = gates[0] if pair == 1 else jnp.concatenate(gates, 1)
        mixed = jnp.dot(exps, block(i, 1), preferred_element_type=jnp.float32)
        total = jnp.dot(exps, ones, preferred_element_type=jnp.float32)
        result = mixed / total * jnp.tanh(gates)
        done(i, g, result.astype(jnp.bfloat16))

    depth = 3
    waiting_scores, waiting_exps = [], []
    for step in range(len(units) + 2 * depth):
        if step < len(units):
            waiting_scores.append(score(*units[step]))
        if depth <= step < len(units) + depth:
            waiting_exps.append(soften(waiting_scores.pop(0)))
        if step >= 2 * depth:
            mix(waiting_exps.pop(0), *units[step - 2 * depth])


def attend_kernel(
    group, pair, early, late, q_ref, kv_ref, gate_ref, *rest
):
    early_ref = rest[0] if early else None
    out_hbm, out_ref, out_sem = rest[-3:]
    head_dim = kv_ref.shape[3]
    groups = len(early) + len(late)
    each = kv_ref.shape[0] // groups
    me = lax.rem(lax.axis_index("seq"), groups)
    copies = []

    def write(src, head, g, wide):
        start = pl.multiple_of(head * (group * head_dim) + g * head_dim, wide)
        copy = pltpu.make_async_copy(
            src, out_hbm.at[:, :, pl.ds(start, wide)], out_sem.at[len(copies)]
        )
        copy.start()
        copies.append(copy)

    block = each * group * head_dim
    for j, k in enumerate(early):
        write(early_ref.at[:, :, j * block : (j + 1) * block], partner(me, k, groups) * each, 0, block)
    heads = [partner(me, k, groups) * each + i for k in late for i in range(each)]
    wide = pair * head_dim

    def done(i, g, result):
        at = slice((i * group + g) * head_dim, (i * group + g) * head_dim + wide)
        out_ref[0, :, at] = result
        write(out_ref.at[:, :, at], heads[i], g, wide)

    attention(group, pair, q_ref, kv_ref, gate_ref, heads, done)
    for copy in copies:
        copy.wait()


def project_kernel(
    sizes,
    plan,
    bundles,
    group,
    pair,
    early,
    vision_ref,
    weight_ref,
    gain_ref,
    query_ref,
    gate_ref,
    kv_ref,
    staged_ref,
    *rest,
):
    early_ref = rest[0] if early else None
    scratch = rest[1:] if early else rest
    return project_steps(
        sizes, plan, bundles, group, pair, early, vision_ref, weight_ref, gain_ref, query_ref, gate_ref,
        kv_ref, staged_ref, early_ref, *scratch
    )


def project_steps(
    sizes,
    plan,
    bundles,
    group,
    pair,
    early,
    vision_ref,
    weight_ref,
    gain_ref,
    query_ref,
    gate_ref,
    kv_ref,
    staged_ref,
    early_ref,
    seen,
    weights,
    gain,
    partial,
    landed,
    ready,
    gate,
    load_sem,
    far_send,
    chip_send,
    pass_send,
    seen_sem,
    sum_send,
    sum_recv,
    kv_send,
    kv_recv,
    in_s,
    in_q,
    in_t,
):
    n_s, n_q, n_t = sizes
    s, q, t = lax.axis_index("section"), lax.axis_index("seq"), lax.axis_index("tp")
    inner, head_dim = kv_ref.shape[0], kv_ref.shape[3]
    stages = len(plan)
    shard = seen.shape[2]
    groups = math.gcd(inner, n_q)
    each = inner // groups
    blocks = n_q // groups
    part = n_t * shard // blocks
    width = each * 2 * head_dim
    half = n_s // 2 if n_s % 2 == 0 else n_s
    last = n_t - 1

    def section_of(k):
        base = (s // half) * half
        return lax.rem(base + (k // half) * half, n_s) + lax.rem(s + k, half)

    def at_device(peer):
        return tuple(0 * s + c if isinstance(c, int) else c for c in peer)

    def signal(sem, peer):
        pl.semaphore_signal(sem, inc=1, device_id=at_device(peer), device_id_type=MESH)

    own = pltpu.make_async_copy(vision_ref, seen.at[s, t], load_sem.at[0])
    load = pltpu.make_async_copy(weight_ref.at[0], weights, load_sem.at[1])
    load_gain = pltpu.make_async_copy(gain_ref, gain, load_sem.at[2])
    stage_queries = pltpu.make_async_copy(query_ref, staged_ref, load_sem.at[3])
    load_gate = pltpu.make_async_copy(gate_ref, gate, load_sem.at[4])

    barrier = pltpu.get_barrier_semaphore()
    for o in range(1, n_s):
        for p in range(n_t):
            @pl.when((o > s) & ((t == 0) | (p == 0)))
            def _():
                signal(barrier, (o, q, p))
    for o in range(1, n_q):
        for p in range(n_t):
            @pl.when((o > q) & ((t == last) | (p == last)))
            def _():
                signal(barrier, (s, o, p))
    for p in range(1, n_t):
        @pl.when(p > t)
        def _():
            signal(barrier, (s, q, p))
    own.start()
    load.start()
    load_gain.start()
    load_gate.start()
    stage_queries.start()
    earlier = s * jnp.where(t == 0, n_t, 1) + q * jnp.where(t == last, n_t, 1) + t

    @pl.when(earlier > 0)
    def _():
        pl.semaphore_wait(barrier, earlier)

    sent = []

    def start(build, when=None):
        def make():
            src, dst, send_sem, recv_sem, peer = build()
            return pltpu.make_async_remote_copy(
                src_ref=src,
                dst_ref=dst,
                send_sem=send_sem,
                recv_sem=recv_sem,
                device_id=at_device(peer),
                device_id_type=MESH,
            )

        if when is None:
            make().start()
        else:
            @pl.when(when)
            def _():
                make().start()
        sent.append((make, when))

    def send(src, dst, send_sem, recv_sem, peer, when=None):
        start(lambda: (src, dst, send_sem, recv_sem, peer), when)

    def arrived(dst, sem):
        pltpu.make_async_copy(dst, dst, sem).wait()

    def far(o, when):
        send(seen.at[s, t], seen.at[s, t], far_send.at[o], seen_sem.at[s, t], (o, q, 0), when)

    own.wait()
    for o in range(n_s - 1):
        for p in range(n_t):
            @pl.when((o < s) & (t == 0))
            def _():
                signal(in_s.at[s], (o, q, p))
    for p in range(n_t - 1):
        @pl.when(p < t)
        def _():
            signal(in_t.at[t], (s, q, p))
    for o in range(n_q - 1):
        for p in range(n_t):
            @pl.when((o < q) & ((t == last) | (p == last)))
            def _():
                signal(in_q.at[q, t], (s, o, p))
    for o in range(n_s - 2):
        far(o, (o < s) & (s < n_s - 1))
    far(n_s - 2, s == n_s - 1)
    for p in range(n_t):
        @pl.when(p > t)
        def _():
            pl.semaphore_wait(in_t.at[p], 1)
        send(seen.at[s, t], seen.at[s, t], chip_send.at[p], seen_sem.at[s, t], (s, q, p), p != t)
    @pl.when(s == n_s - 1)
    def _():
        for p in range(n_t):
            @pl.when(p != t)
            def _():
                arrived(seen.at[s, p], seen_sem.at[s, p])
    if n_s > 2:
        far(0, s == n_s - 1)

    def upward():
        for o in range(1, n_s):
            @pl.when(o > s)
            def _():
                pl.semaphore_wait(in_s.at[o], 1)
            far(o, o > s)

    def project(stage):
        for k in plan[stage]:
            if k > 0:
                sec = section_of(k)
                for p in range(n_t):
                    arrived(seen.at[sec, p], seen_sem.at[sec, p])
                    for o in range(1, n_t):
                        send(
                            seen.at[sec, p],
                            seen.at[sec, p],
                            pass_send.at[k, p, o],
                            seen_sem.at[sec, p],
                            (s, q, o),
                            t == 0,
                        )
            else:
                for p in range(n_t):
                    @pl.when((p != t) & (s < n_s - 1))
                    def _():
                        arrived(seen.at[s, p], seen_sem.at[s, p])
        if stage == 0:
            load.wait()
        parts = [
            seen[section_of(k) if k else s].reshape(n_t * shard, seen.shape[3])
            for k in plan[stage]
        ]
        share = len(parts) * part
        first = plan[stage][0] * part
        rows_at = pl.ds(first, share)
        block = parts[0] if len(parts) == 1 else jnp.concatenate(parts, 0)
        for k in range(groups - 1, -1, -1):
            g = partner(lax.rem(q, groups), k, groups)
            at = pl.ds(pl.multiple_of(g * width, width), width)
            product = jnp.dot(block, weights[:, at], preferred_element_type=jnp.float32)
            for b in range(blocks):
                o = b * groups + g
                partial[o, rows_at] = product[b * share : (b + 1) * share]
                if stage == 0:
                    @pl.when(o > q)
                    def _():
                        pl.semaphore_wait(in_q.at[o, last], 1)
                send(
                    partial.at[o, rows_at],
                    landed.at[t, q, rows_at],
                    sum_send.at[stage, o],
                    sum_recv.at[stage, t, q],
                    (s, o, last),
                    (o != q) | (t != last),
                )

    def span(bundle):
        first = plan[bundle[0]][0] * part
        return first, sum(len(plan[stage]) for stage in bundle) * part

    def place(bundle, o):
        share = span(bundle)[1]
        row = plan[bundle[0]][0] * n_t * shard + (o // groups) * share
        if not isinstance(o, int):
            row = pl.multiple_of(row, share)
        return pl.ds(o % groups * each, each), pl.ds(row, share)

    others = [partner(q, k, n_q) if groups == n_q else lax.rem(q + k, n_q) for k in range(n_q)]
    mine_at = [place(bundle, q) for bundle in bundles]

    def finish(stage):
        own_at = pl.ds(plan[stage][0] * part, len(plan[stage]) * part)
        for p in range(n_t):
            for k in range(n_q):
                o = lax.rem(q + k, n_q)
                if p != last or k > 0:
                    arrived(landed.at[p, o, own_at], sum_recv.at[stage, p, o])
            for h in range(each):
                at_k = slice(2 * h * head_dim, (2 * h + 1) * head_dim)
                at_v = slice((2 * h + 1) * head_dim, (2 * h + 2) * head_dim)
                mine = partial.at[q] if p == last else landed.at[p, q]
                raw_k, raw_v = mine[own_at, at_k], mine[own_at, at_v]
                for k in range(1, n_q):
                    o = lax.rem(q + k, n_q)
                    raw_k += landed[p, o, own_at, at_k]
                    raw_v += landed[p, o, own_at, at_v]
                mean = jnp.mean(raw_k * raw_k, axis=-1, keepdims=True)
                scaled = raw_k * lax.rsqrt(mean + eps_norm) * gain[...]
                ready[p, h, 0, own_at] = scaled.astype(jnp.bfloat16)
                ready[p, h, 1, own_at] = raw_v.astype(jnp.bfloat16)
            closing = [b for b, bundle in enumerate(bundles) if bundle[-1] == stage]
            for b in closing:
                deliver(b, p)

    def deliver(b, p):
        heads_at, rows_at = mine_at[b]
        sent_at = pl.ds(*span(bundles[b]))
        for k in range(n_q - 1, -1, -1):
            if k == 0 and p == last:
                kv_ref[heads_at, :, rows_at, :] = ready[p, :, :, sent_at]
                continue
            o = others[k]
            if b == 0 and p != last and k > 0:
                @pl.when(o > q)
                def _():
                    pl.semaphore_wait(in_q.at[o, p], 1)
            start(
                lambda p=p, o=o: (
                    ready.at[p, :, :, sent_at],
                    kv_ref.at[heads_at, :, rows_at, :],
                    kv_send.at[b, p, o],
                    kv_recv.at[b, q],
                    (s, o, p),
                )
            )

    def owner(step):
        before = len(sent)

        @pl.when(t == last)
        def _():
            step()
        sent[before:] = [(make, t == last) for make, _ in sent[before:]]

    def collect(b, o):
        heads_at, rows_at = place(bundles[b], o)

        @pl.when((o != q) | (t != last))
        def _():
            arrived(kv_ref.at[heads_at, :, rows_at, :], kv_recv.at[b, o])

    def attend_early(j):
        def done(i, g, result):
            at = ((j * each + i) * group + g) * head_dim
            early_ref[0, :, at : at + pair * head_dim] = result

        first_head = partner(lax.rem(q, groups), early[j], groups) * each
        heads = [first_head + i for i in range(each)]
        attention(group, pair, staged_ref, kv_ref, gate, heads, done)

    load_gain.wait()
    upward()
    for stage in range(stages):
        project(stage)
        if stage == 0:
            for o in range(1, n_s - 2):
                far(o, s == n_s - 1)
        if stage >= 2:
            owner(functools.partial(finish, stage - 2))
    for stage in range(max(stages - 2, 0), stages):
        owner(functools.partial(finish, stage))
    stage_queries.wait()
    load_gate.wait()
    for j in range(len(early)):
        for b in range(len(bundles)):
            collect(b, others[early[j]])
        attend_early(j)
    for k in range(n_q):
        if k not in early:
            for b in range(len(bundles)):
                collect(b, others[k])
    for make, when in sent:
        if when is None:
            make().wait_send()
        else:
            @pl.when(when)
            def _():
                make().wait_send()


def local(sizes, queries, vision, kv_weight, key_gain, head_gate):
    n_s, n_q, n_t = sizes
    head_dim = key_gain.shape[1]
    shard, features = vision.shape
    columns = kv_weight.shape[2]
    rows = shard * n_s * n_t
    inner = columns // (2 * head_dim)
    blocks = n_q // math.gcd(inner, n_q)
    step = max(n_s // 4, 1)
    while step < n_s and step * n_t * shard % (16 * blocks):
        step += 1
    cuts = [k for k in (0, step, 2 * step) if k < n_s] + [n_s]
    plan = [list(range(a, b)) for a, b in zip(cuts, cuts[1:])]
    stages = len(plan)
    bundles = [list(range(stages - 1)), [stages - 1]] if blocks == 1 else [[i] for i in range(stages)]
    each = inner // math.gcd(inner, n_q)
    hbm = pl.BlockSpec(memory_space=pltpu.HBM)
    vmem = pl.BlockSpec(memory_space=pltpu.VMEM)
    dma = pltpu.SemaphoreType.DMA
    regular = pltpu.SemaphoreType.REGULAR
    heads = head_gate.shape[1]
    group = heads // inner
    pair = 2 if group % 2 == 0 and rows == head_dim else 1
    groups = n_q // blocks
    early = (0,) if blocks == 1 else ()
    late = tuple(k for k in range(groups) if k not in early)
    ahead = [pltpu.VMEM(queries.shape[:2] + (len(early) * each * group * head_dim,), jnp.bfloat16)]
    ahead = ahead if early else []
    smem = pl.BlockSpec(memory_space=pltpu.SMEM)
    kv, staged, *ahead = pl.pallas_call(
        functools.partial(project_kernel, sizes, plan, bundles, group, pair, early),
        out_shape=(
            pltpu.VMEM((inner, 2, rows, head_dim), jnp.bfloat16),
            pltpu.VMEM(queries.shape, jnp.bfloat16),
            *ahead,
        ),
        in_specs=[hbm] * 5,
        out_specs=(vmem, vmem) + (vmem,) * len(ahead),
        scratch_shapes=[
            pltpu.VMEM((n_s, n_t, shard, features), jnp.bfloat16),
            pltpu.VMEM((features, columns), jnp.bfloat16),
            pltpu.VMEM(key_gain.shape, jnp.float32),
            pltpu.VMEM((n_q, rows // blocks, each * 2 * head_dim), jnp.float32),
            pltpu.VMEM((n_t, n_q, rows // blocks, each * 2 * head_dim), jnp.float32),
            pltpu.VMEM((n_t, each, 2, rows // blocks, head_dim), jnp.bfloat16),
            pltpu.SMEM(head_gate.shape, jnp.float32),
            dma((5,)),
            dma((n_s,)),
            dma((n_t,)),
            dma((n_s, n_t, n_t)),
            dma((n_s, n_t)),
            dma((stages, n_q)),
            dma((stages, n_t, n_q)),
            dma((stages, n_t, n_q)),
            dma((stages, n_q)),
            regular((n_s,)),
            regular((n_q, n_t)),
            regular((n_t,)),
        ],
        compiler_params=pltpu.CompilerParams(
            collective_id=0, has_side_effects=True, vmem_limit_bytes=24 << 20
        ),
        name="project",
    )(
        *[
            pltpu.with_memory_space_constraint(x, pltpu.HBM)
            for x in (vision, kv_weight, key_gain, queries, head_gate)
        ]
    )

    return pl.pallas_call(
        functools.partial(attend_kernel, group, pair, early, late),
        out_shape=jax.ShapeDtypeStruct(queries.shape, jnp.bfloat16),
        in_specs=[vmem, vmem, smem] + [vmem] * len(ahead),
        out_specs=hbm,
        scratch_shapes=[
            pltpu.VMEM(queries.shape[:2] + (len(late) * each * group * head_dim,), jnp.bfloat16),
            dma((len(early) + len(late) * each * group // pair,)),
        ],
        compiler_params=pltpu.CompilerParams(vmem_limit_bytes=24 << 20),
        name="attend",
    )(staged, kv, head_gate, *ahead)


def solution(mesh):
    sizes = tuple(mesh.shape[name] for name in ("section", "seq", "tp"))
    return jax.shard_map(
        functools.partial(local, sizes),
        mesh=mesh,
        in_specs=(
            P("section", "seq", "tp"),
            P(("section", "tp"), "seq"),
            P("section", "seq", "tp"),
            P("section", None),
            P("section", "tp"),
        ),
        out_specs=P("section", "seq", "tp"),
        check_vma=False,
    )
```

```python
import functools
import math

import jax
import jax.numpy as jnp
from jax import lax
from jax.experimental import pallas as pl
from jax.experimental.pallas import tpu as pltpu
from jax.sharding import PartitionSpec as P

MESH = pl.DeviceIdType.MESH
eps_norm = 1e-05


def partner(i, k, n):
    if n & (n - 1):
        return lax.rem(i + k, n)
    result, bit = i, 1
    while bit < n:
        if k & bit:
            result = result + bit - 2 * bit * ((i // bit) % 2)
        bit *= 2
    return result


def attention(group, pair, q_ref, kv_ref, gate_ref, heads, done):
    _, _, rows, head_dim = kv_ref.shape
    scale = head_dim ** (-0.5)

    def diagonal(block):
        if pair == 1:
            return block
        zero = jnp.zeros_like(block)
        return jnp.concatenate(
            [jnp.concatenate([block, zero], 1), jnp.concatenate([zero, block], 1)], 0
        )

    ones = diagonal(jnp.ones((rows, head_dim), jnp.bfloat16))
    made = {}

    def block(i, kind):
        if (i, kind) not in made:
            made[i, kind] = diagonal(kv_ref[heads[i], kind])
        return made[i, kind]

    wide = pair * head_dim
    units = [(i, g) for i in range(len(heads)) for g in range(0, group, pair)]

    def score(i, g):
        start = pl.multiple_of(heads[i] * (group * head_dim) + g * head_dim, wide)
        return lax.dot_general(
            q_ref[0, :, pl.ds(start, wide)],
            block(i, 0),
            (((1,), (1,)), ((), ())),
            preferred_element_type=jnp.float32,
        )

    def soften(scores):
        exps = []
        for p in range(pair):
            part = scores[:, p * rows : (p + 1) * rows]
            peak = jnp.max(part, axis=-1, keepdims=True)
            exps.append(jnp.exp((part - peak) * scale).astype(jnp.bfloat16))
        return exps[0] if pair == 1 else jnp.concatenate(exps, 1)

    def mix(exps, i, g):
        gates = [
            jnp.full((1, head_dim), gate_ref[0, heads[i] * group + g + p]) for p in range(pair)
        ]
        gates = gates[0] if pair == 1 else jnp.concatenate(gates, 1)
        mixed = jnp.dot(exps, block(i, 1), preferred_element_type=jnp.float32)
        total = jnp.dot(exps, ones, preferred_element_type=jnp.float32)
        result = mixed / total * jnp.tanh(gates)
        done(i, g, result.astype(jnp.bfloat16))

    depth = 3
    waiting_scores, waiting_exps = [], []
    for step in range(len(units) + 2 * depth):
        if step < len(units):
            waiting_scores.append(score(*units[step]))
        if depth <= step < len(units) + depth:
            waiting_exps.append(soften(waiting_scores.pop(0)))
        if step >= 2 * depth:
            mix(waiting_exps.pop(0), *units[step - 2 * depth])


def attend_kernel(
    group, pair, early, late, q_ref, kv_ref, gate_ref, *rest
):
    early_ref = rest[0] if early else None
    out_hbm, out_ref, out_sem = rest[-3:]
    head_dim = kv_ref.shape[3]
    groups = len(early) + len(late)
    each = kv_ref.shape[0] // groups
    me = lax.rem(lax.axis_index("seq"), groups)
    copies = []

    def write(src, head, g, wide):
        start = pl.multiple_of(head * (group * head_dim) + g * head_dim, wide)
        copy = pltpu.make_async_copy(
            src, out_hbm.at[:, :, pl.ds(start, wide)], out_sem.at[len(copies)]
        )
        copy.start()
        copies.append(copy)

    block = each * group * head_dim
    for j, k in enumerate(early):
        write(early_ref.at[:, :, j * block : (j + 1) * block], partner(me, k, groups) * each, 0, block)
    heads = [partner(me, k, groups) * each + i for k in late for i in range(each)]
    wide = pair * head_dim

    def done(i, g, result):
        at = slice((i * group + g) * head_dim, (i * group + g) * head_dim + wide)
        out_ref[0, :, at] = result
        write(out_ref.at[:, :, at], heads[i], g, wide)

    attention(group, pair, q_ref, kv_ref, gate_ref, heads, done)
    for copy in copies:
        copy.wait()


def project_kernel(
    sizes,
    plan,
    bundles,
    group,
    pair,
    early,
    vision_ref,
    weight_ref,
    gain_ref,
    query_ref,
    gate_ref,
    kv_ref,
    staged_ref,
    *rest,
):
    early_ref = rest[0] if early else None
    scratch = rest[1:] if early else rest
    return project_steps(
        sizes, plan, bundles, group, pair, early, vision_ref, weight_ref, gain_ref, query_ref, gate_ref,
        kv_ref, staged_ref, early_ref, *scratch
    )


def project_steps(
    sizes,
    plan,
    bundles,
    group,
    pair,
    early,
    vision_ref,
    weight_ref,
    gain_ref,
    query_ref,
    gate_ref,
    kv_ref,
    staged_ref,
    early_ref,
    seen,
    weights,
    gain,
    partial,
    landed,
    ready,
    gate,
    load_sem,
    far_send,
    chip_send,
    pass_send,
    seen_sem,
    sum_send,
    sum_recv,
    kv_send,
    kv_recv,
    in_s,
    in_q,
    in_t,
):
    n_s, n_q, n_t = sizes
    s, q, t = lax.axis_index("section"), lax.axis_index("seq"), lax.axis_index("tp")
    inner, head_dim = kv_ref.shape[0], kv_ref.shape[3]
    stages = len(plan)
    shard = seen.shape[2]
    groups = math.gcd(inner, n_q)
    each = inner // groups
    blocks = n_q // groups
    part = n_t * shard // blocks
    width = each * 2 * head_dim
    half = n_s // 2 if n_s % 2 == 0 else n_s
    last = n_t - 1

    def section_of(k):
        base = (s // half) * half
        return lax.rem(base + (k // half) * half, n_s) + lax.rem(s + k, half)

    def at_device(peer):
        return tuple(0 * s + c if isinstance(c, int) else c for c in peer)

    def signal(sem, peer):
        pl.semaphore_signal(sem, inc=1, device_id=at_device(peer), device_id_type=MESH)

    own = pltpu.make_async_copy(vision_ref, seen.at[s, t], load_sem.at[0])
    load = pltpu.make_async_copy(weight_ref.at[0], weights, load_sem.at[1])
    load_gain = pltpu.make_async_copy(gain_ref, gain, load_sem.at[2])
    stage_queries = pltpu.make_async_copy(query_ref, staged_ref, load_sem.at[3])
    load_gate = pltpu.make_async_copy(gate_ref, gate, load_sem.at[4])

    barrier = pltpu.get_barrier_semaphore()
    for o in range(1, n_s):
        for p in range(n_t):
            @pl.when((o > s) & ((t == 0) | (p == 0)))
            def _():
                signal(barrier, (o, q, p))
    for o in range(1, n_q):
        for p in range(n_t):
            @pl.when((o > q) & ((t == last) | (p == last)))
            def _():
                signal(barrier, (s, o, p))
    for p in range(1, n_t):
        @pl.when(p > t)
        def _():
            signal(barrier, (s, q, p))
    own.start()
    load.start()
    load_gain.start()
    load_gate.start()
    stage_queries.start()
    earlier = s * jnp.where(t == 0, n_t, 1) + q * jnp.where(t == last, n_t, 1) + t

    @pl.when(earlier > 0)
    def _():
        pl.semaphore_wait(barrier, earlier)

    sent = []

    def start(build, when=None):
        def make():
            src, dst, send_sem, recv_sem, peer = build()
            return pltpu.make_async_remote_copy(
                src_ref=src,
                dst_ref=dst,
                send_sem=send_sem,
                recv_sem=recv_sem,
                device_id=at_device(peer),
                device_id_type=MESH,
            )

        if when is None:
            make().start()
        else:
            @pl.when(when)
            def _():
                make().start()
        sent.append((make, when))

    def send(src, dst, send_sem, recv_sem, peer, when=None):
        start(lambda: (src, dst, send_sem, recv_sem, peer), when)

    def arrived(dst, sem):
        pltpu.make_async_copy(dst, dst, sem).wait()

    def far(o, when):
        send(seen.at[s, t], seen.at[s, t], far_send.at[o], seen_sem.at[s, t], (o, q, 0), when)

    own.wait()
    for o in range(n_s - 1):
        for p in range(n_t):
            @pl.when((o < s) & (t == 0))
            def _():
                signal(in_s.at[s], (o, q, p))
    for p in range(n_t - 1):
        @pl.when(p < t)
        def _():
            signal(in_t.at[t], (s, q, p))
    for o in range(n_q - 1):
        for p in range(n_t):
            @pl.when((o < q) & ((t == last) | (p == last)))
            def _():
                signal(in_q.at[q, t], (s, o, p))
    for o in range(n_s - 2):
        far(o, (o < s) & (s < n_s - 1))
    far(n_s - 2, s == n_s - 1)
    for p in range(n_t):
        @pl.when(p > t)
        def _():
            pl.semaphore_wait(in_t.at[p], 1)
        send(seen.at[s, t], seen.at[s, t], chip_send.at[p], seen_sem.at[s, t], (s, q, p), p != t)
    @pl.when(s == n_s - 1)
    def _():
        for p in range(n_t):
            @pl.when(p != t)
            def _():
                arrived(seen.at[s, p], seen_sem.at[s, p])
    if n_s > 2:
        far(0, s == n_s - 1)

    def upward():
        for o in range(1, n_s):
            @pl.when(o > s)
            def _():
                pl.semaphore_wait(in_s.at[o], 1)
            far(o, o > s)

    def project(stage):
        for k in plan[stage]:
            if k > 0:
                sec = section_of(k)
                @pl.when(t == 0)
                def _():
                    for p in range(n_t):
                        arrived(seen.at[sec, p], seen_sem.at[sec, p])
                for o in range(1, n_t):
                    send(
                        seen.at[sec],
                        seen.at[sec],
                        pass_send.at[k, 0, o],
                        seen_sem.at[sec, 0],
                        (s, q, o),
                        t == 0,
                    )

                @pl.when(t != 0)
                def _():
                    arrived(seen.at[sec], seen_sem.at[sec, 0])
            else:
                for p in range(n_t):
                    @pl.when((p != t) & (s < n_s - 1))
                    def _():
                        arrived(seen.at[s, p], seen_sem.at[s, p])
        if stage == 0:
            load.wait()
        parts = [
            seen[section_of(k) if k else s].reshape(n_t * shard, seen.shape[3])
            for k in plan[stage]
        ]
        share = len(parts) * part
        first = plan[stage][0] * part
        rows_at = pl.ds(first, share)
        block = parts[0] if len(parts) == 1 else jnp.concatenate(parts, 0)
        for k in range(groups - 1, -1, -1):
            g = partner(lax.rem(q, groups), k, groups)
            at = pl.ds(pl.multiple_of(g * width, width), width)
            product = jnp.dot(block, weights[:, at], preferred_element_type=jnp.float32)
            for b in range(blocks):
                o = b * groups + g
                partial[o, rows_at] = product[b * share : (b + 1) * share]
                if stage == 0:
                    @pl.when(o > q)
                    def _():
                        pl.semaphore_wait(in_q.at[o, last], 1)
                send(
                    partial.at[o, rows_at],
                    landed.at[t, q, rows_at],
                    sum_send.at[stage, o],
                    sum_recv.at[stage, t, q],
                    (s, o, last),
                    (o != q) | (t != last),
                )

    def span(bundle):
        first = plan[bundle[0]][0] * part
        return first, sum(len(plan[stage]) for stage in bundle) * part

    def place(bundle, o):
        share = span(bundle)[1]
        row = plan[bundle[0]][0] * n_t * shard + (o // groups) * share
        if not isinstance(o, int):
            row = pl.multiple_of(row, share)
        return pl.ds(o % groups * each, each), pl.ds(row, share)

    others = [partner(q, k, n_q) if groups == n_q else lax.rem(q + k, n_q) for k in range(n_q)]
    mine_at = [place(bundle, q) for bundle in bundles]

    def finish(stage):
        own_at = pl.ds(plan[stage][0] * part, len(plan[stage]) * part)
        for p in range(n_t):
            for k in range(n_q):
                o = lax.rem(q + k, n_q)
                if p != last or k > 0:
                    arrived(landed.at[p, o, own_at], sum_recv.at[stage, p, o])
            for h in range(each):
                at_k = slice(2 * h * head_dim, (2 * h + 1) * head_dim)
                at_v = slice((2 * h + 1) * head_dim, (2 * h + 2) * head_dim)
                mine = partial.at[q] if p == last else landed.at[p, q]
                raw_k, raw_v = mine[own_at, at_k], mine[own_at, at_v]
                for k in range(1, n_q):
                    o = lax.rem(q + k, n_q)
                    raw_k += landed[p, o, own_at, at_k]
                    raw_v += landed[p, o, own_at, at_v]
                mean = jnp.mean(raw_k * raw_k, axis=-1, keepdims=True)
                scaled = raw_k * lax.rsqrt(mean + eps_norm) * gain[...]
                ready[p, h, 0, own_at] = scaled.astype(jnp.bfloat16)
                ready[p, h, 1, own_at] = raw_v.astype(jnp.bfloat16)
            closing = [b for b, bundle in enumerate(bundles) if bundle[-1] == stage]
            for b in closing:
                deliver(b, p)

    def deliver(b, p):
        heads_at, rows_at = mine_at[b]
        sent_at = pl.ds(*span(bundles[b]))
        for k in range(n_q - 1, -1, -1):
            if k == 0 and p == last:
                kv_ref[heads_at, :, rows_at, :] = ready[p, :, :, sent_at]
                continue
            o = others[k]
            if b == 0 and p != last and k > 0:
                @pl.when(o > q)
                def _():
                    pl.semaphore_wait(in_q.at[o, p], 1)
            start(
                lambda p=p, o=o: (
                    ready.at[p, :, :, sent_at],
                    kv_ref.at[heads_at, :, rows_at, :],
                    kv_send.at[b, p, o],
                    kv_recv.at[b, q],
                    (s, o, p),
                )
            )

    def owner(step):
        before = len(sent)

        @pl.when(t == last)
        def _():
            step()
        sent[before:] = [(make, t == last) for make, _ in sent[before:]]

    def collect(b, o):
        heads_at, rows_at = place(bundles[b], o)

        @pl.when((o != q) | (t != last))
        def _():
            arrived(kv_ref.at[heads_at, :, rows_at, :], kv_recv.at[b, o])

    def attend_early(j):
        def done(i, g, result):
            at = ((j * each + i) * group + g) * head_dim
            early_ref[0, :, at : at + pair * head_dim] = result

        first_head = partner(lax.rem(q, groups), early[j], groups) * each
        heads = [first_head + i for i in range(each)]
        attention(group, pair, staged_ref, kv_ref, gate, heads, done)

    load_gain.wait()
    upward()
    for stage in range(stages):
        project(stage)
        if stage == 0:
            for o in range(1, n_s - 2):
                far(o, s == n_s - 1)
        if stage >= 2:
            owner(functools.partial(finish, stage - 2))
    for stage in range(max(stages - 2, 0), stages):
        owner(functools.partial(finish, stage))
    stage_queries.wait()
    load_gate.wait()
    for j in range(len(early)):
        for b in range(len(bundles)):
            collect(b, others[early[j]])
        attend_early(j)
    for k in range(n_q):
        if k not in early:
            for b in range(len(bundles)):
                collect(b, others[k])
    for make, when in sent:
        if when is None:
            make().wait_send()
        else:
            @pl.when(when)
            def _():
                make().wait_send()


def local(sizes, queries, vision, kv_weight, key_gain, head_gate):
    n_s, n_q, n_t = sizes
    head_dim = key_gain.shape[1]
    shard, features = vision.shape
    columns = kv_weight.shape[2]
    rows = shard * n_s * n_t
    inner = columns // (2 * head_dim)
    blocks = n_q // math.gcd(inner, n_q)
    step = max(n_s // 4, 1)
    while step < n_s and step * n_t * shard % (16 * blocks):
        step += 1
    cuts = [k for k in (0, step, 2 * step) if k < n_s] + [n_s]
    plan = [list(range(a, b)) for a, b in zip(cuts, cuts[1:])]
    stages = len(plan)
    bundles = [list(range(stages - 1)), [stages - 1]] if blocks == 1 else [[i] for i in range(stages)]
    each = inner // math.gcd(inner, n_q)
    hbm = pl.BlockSpec(memory_space=pltpu.HBM)
    vmem = pl.BlockSpec(memory_space=pltpu.VMEM)
    dma = pltpu.SemaphoreType.DMA
    regular = pltpu.SemaphoreType.REGULAR
    heads = head_gate.shape[1]
    group = heads // inner
    pair = 2 if group % 2 == 0 and rows == head_dim else 1
    groups = n_q // blocks
    early = (0,) if blocks == 1 else ()
    late = tuple(k for k in range(groups) if k not in early)
    ahead = [pltpu.VMEM(queries.shape[:2] + (len(early) * each * group * head_dim,), jnp.bfloat16)]
    ahead = ahead if early else []
    smem = pl.BlockSpec(memory_space=pltpu.SMEM)
    kv, staged, *ahead = pl.pallas_call(
        functools.partial(project_kernel, sizes, plan, bundles, group, pair, early),
        out_shape=(
            pltpu.VMEM((inner, 2, rows, head_dim), jnp.bfloat16),
            pltpu.VMEM(queries.shape, jnp.bfloat16),
            *ahead,
        ),
        in_specs=[hbm] * 5,
        out_specs=(vmem, vmem) + (vmem,) * len(ahead),
        scratch_shapes=[
            pltpu.VMEM((n_s, n_t, shard, features), jnp.bfloat16),
            pltpu.VMEM((features, columns), jnp.bfloat16),
            pltpu.VMEM(key_gain.shape, jnp.float32),
            pltpu.VMEM((n_q, rows // blocks, each * 2 * head_dim), jnp.float32),
            pltpu.VMEM((n_t, n_q, rows // blocks, each * 2 * head_dim), jnp.float32),
            pltpu.VMEM((n_t, each, 2, rows // blocks, head_dim), jnp.bfloat16),
            pltpu.SMEM(head_gate.shape, jnp.float32),
            dma((5,)),
            dma((n_s,)),
            dma((n_t,)),
            dma((n_s, n_t, n_t)),
            dma((n_s, n_t)),
            dma((stages, n_q)),
            dma((stages, n_t, n_q)),
            dma((stages, n_t, n_q)),
            dma((stages, n_q)),
            regular((n_s,)),
            regular((n_q, n_t)),
            regular((n_t,)),
        ],
        compiler_params=pltpu.CompilerParams(
            collective_id=0, has_side_effects=True, vmem_limit_bytes=24 << 20
        ),
        name="project",
    )(
        *[
            pltpu.with_memory_space_constraint(x, pltpu.HBM)
            for x in (vision, kv_weight, key_gain, queries, head_gate)
        ]
    )

    return pl.pallas_call(
        functools.partial(attend_kernel, group, pair, early, late),
        out_shape=jax.ShapeDtypeStruct(queries.shape, jnp.bfloat16),
        in_specs=[vmem, vmem, smem] + [vmem] * len(ahead),
        out_specs=hbm,
        scratch_shapes=[
            pltpu.VMEM(queries.shape[:2] + (len(late) * each * group * head_dim,), jnp.bfloat16),
            dma((len(early) + len(late) * each * group // pair,)),
        ],
        compiler_params=pltpu.CompilerParams(vmem_limit_bytes=24 << 20),
        name="attend",
    )(staged, kv, head_gate, *ahead)


def solution(mesh):
    sizes = tuple(mesh.shape[name] for name in ("section", "seq", "tp"))
    return jax.shard_map(
        functools.partial(local, sizes),
        mesh=mesh,
        in_specs=(
            P("section", "seq", "tp"),
            P(("section", "tp"), "seq"),
            P("section", "seq", "tp"),
            P("section", None),
            P("section", "tp"),
        ),
        out_specs=P("section", "seq", "tp"),
        check_vma=False,
    )
```

```python
import functools
import math

import jax
import jax.numpy as jnp
from jax import lax
from jax.experimental import pallas as pl
from jax.experimental.pallas import tpu as pltpu
from jax.sharding import PartitionSpec as P

MESH = pl.DeviceIdType.MESH
eps_norm = 1e-05


def partner(i, k, n):
    if n & (n - 1):
        return lax.rem(i + k, n)
    result, bit = i, 1
    while bit < n:
        if k & bit:
            result = result + bit - 2 * bit * ((i // bit) % 2)
        bit *= 2
    return result


def attention(group, pair, q_ref, kv_ref, gate_ref, heads, done):
    _, _, rows, head_dim = kv_ref.shape
    scale = head_dim ** (-0.5)

    def diagonal(block):
        if pair == 1:
            return block
        zero = jnp.zeros_like(block)
        return jnp.concatenate(
            [jnp.concatenate([block, zero], 1), jnp.concatenate([zero, block], 1)], 0
        )

    ones = diagonal(jnp.ones((rows, head_dim), jnp.bfloat16))
    made = {}

    def block(i, kind):
        if (i, kind) not in made:
            made[i, kind] = diagonal(kv_ref[heads[i], kind])
        return made[i, kind]

    wide = pair * head_dim
    units = [(i, g) for i in range(len(heads)) for g in range(0, group, pair)]

    def score(i, g):
        start = pl.multiple_of(heads[i] * (group * head_dim) + g * head_dim, wide)
        return lax.dot_general(
            q_ref[0, :, pl.ds(start, wide)],
            block(i, 0),
            (((1,), (1,)), ((), ())),
            preferred_element_type=jnp.float32,
        )

    def soften(scores):
        exps = []
        for p in range(pair):
            part = scores[:, p * rows : (p + 1) * rows]
            peak = jnp.max(part, axis=-1, keepdims=True)
            exps.append(jnp.exp((part - peak) * scale).astype(jnp.bfloat16))
        return exps[0] if pair == 1 else jnp.concatenate(exps, 1)

    def mix(exps, i, g):
        gates = [
            jnp.full((1, head_dim), gate_ref[0, heads[i] * group + g + p]) for p in range(pair)
        ]
        gates = gates[0] if pair == 1 else jnp.concatenate(gates, 1)
        mixed = jnp.dot(exps, block(i, 1), preferred_element_type=jnp.float32)
        total = jnp.dot(exps, ones, preferred_element_type=jnp.float32)
        result = mixed / total * jnp.tanh(gates)
        done(i, g, result.astype(jnp.bfloat16))

    depth = 3
    waiting_scores, waiting_exps = [], []
    for step in range(len(units) + 2 * depth):
        if step < len(units):
            waiting_scores.append(score(*units[step]))
        if depth <= step < len(units) + depth:
            waiting_exps.append(soften(waiting_scores.pop(0)))
        if step >= 2 * depth:
            mix(waiting_exps.pop(0), *units[step - 2 * depth])


def attend_kernel(
    group, pair, early, late, q_ref, kv_ref, gate_ref, *rest
):
    early_ref = rest[0] if early else None
    out_hbm, out_ref, out_sem = rest[-3:]
    head_dim = kv_ref.shape[3]
    groups = len(early) + len(late)
    each = kv_ref.shape[0] // groups
    me = lax.rem(lax.axis_index("seq"), groups)
    copies = []

    def write(src, head, g, wide):
        start = pl.multiple_of(head * (group * head_dim) + g * head_dim, wide)
        copy = pltpu.make_async_copy(
            src, out_hbm.at[:, :, pl.ds(start, wide)], out_sem.at[len(copies)]
        )
        copy.start()
        copies.append(copy)

    block = each * group * head_dim
    for j, k in enumerate(early):
        write(early_ref.at[:, :, j * block : (j + 1) * block], partner(me, k, groups) * each, 0, block)
    heads = [partner(me, k, groups) * each + i for k in late for i in range(each)]
    wide = pair * head_dim

    def done(i, g, result):
        at = slice((i * group + g) * head_dim, (i * group + g) * head_dim + wide)
        out_ref[0, :, at] = result
        write(out_ref.at[:, :, at], heads[i], g, wide)

    attention(group, pair, q_ref, kv_ref, gate_ref, heads, done)
    for copy in copies:
        copy.wait()


def project_kernel(
    sizes,
    plan,
    bundles,
    group,
    pair,
    early,
    vision_ref,
    weight_ref,
    gain_ref,
    query_ref,
    gate_ref,
    kv_ref,
    staged_ref,
    *rest,
):
    early_ref = rest[0] if early else None
    scratch = rest[1:] if early else rest
    return project_steps(
        sizes, plan, bundles, group, pair, early, vision_ref, weight_ref, gain_ref, query_ref, gate_ref,
        kv_ref, staged_ref, early_ref, *scratch
    )


def project_steps(
    sizes,
    plan,
    bundles,
    group,
    pair,
    early,
    vision_ref,
    weight_ref,
    gain_ref,
    query_ref,
    gate_ref,
    kv_ref,
    staged_ref,
    early_ref,
    seen,
    weights,
    gain,
    partial,
    landed,
    ready,
    gate,
    load_sem,
    far_send,
    chip_send,
    pass_send,
    seen_sem,
    sum_send,
    sum_recv,
    kv_send,
    kv_recv,
    in_s,
    in_q,
    in_t,
):
    n_s, n_q, n_t = sizes
    s, q, t = lax.axis_index("section"), lax.axis_index("seq"), lax.axis_index("tp")
    inner, head_dim = kv_ref.shape[0], kv_ref.shape[3]
    stages = len(plan)
    shard = seen.shape[2]
    groups = math.gcd(inner, n_q)
    each = inner // groups
    blocks = n_q // groups
    part = n_t * shard // blocks
    width = each * 2 * head_dim
    half = n_s // 2 if n_s % 2 == 0 else n_s
    last = n_t - 1

    def section_of(k):
        base = (s // half) * half
        return lax.rem(base + (k // half) * half, n_s) + lax.rem(s + k, half)

    def at_device(peer):
        return tuple(0 * s + c if isinstance(c, int) else c for c in peer)

    def signal(sem, peer):
        pl.semaphore_signal(sem, inc=1, device_id=at_device(peer), device_id_type=MESH)

    own = pltpu.make_async_copy(vision_ref, seen.at[s, t], load_sem.at[0])
    load = pltpu.make_async_copy(weight_ref.at[0], weights, load_sem.at[1])
    load_gain = pltpu.make_async_copy(gain_ref, gain, load_sem.at[2])
    stage_queries = pltpu.make_async_copy(query_ref, staged_ref, load_sem.at[3])
    load_gate = pltpu.make_async_copy(gate_ref, gate, load_sem.at[4])

    barrier = pltpu.get_barrier_semaphore()
    for o in range(1, n_s):
        for p in range(n_t):
            @pl.when((o > s) & ((t == 0) | (p == 0)))
            def _():
                signal(barrier, (o, q, p))
    for o in range(1, n_q):
        for p in range(n_t):
            @pl.when((o > q) & ((t == last) | (p == last)))
            def _():
                signal(barrier, (s, o, p))
    for p in range(1, n_t):
        @pl.when(p > t)
        def _():
            signal(barrier, (s, q, p))
    own.start()
    load.start()
    load_gain.start()
    load_gate.start()
    stage_queries.start()
    earlier = s * jnp.where(t == 0, n_t, 1) + q * jnp.where(t == last, n_t, 1) + t

    @pl.when(earlier > 0)
    def _():
        pl.semaphore_wait(barrier, earlier)

    sent = []

    def start(build, when=None):
        def make():
            src, dst, send_sem, recv_sem, peer = build()
            return pltpu.make_async_remote_copy(
                src_ref=src,
                dst_ref=dst,
                send_sem=send_sem,
                recv_sem=recv_sem,
                device_id=at_device(peer),
                device_id_type=MESH,
            )

        if when is None:
            make().start()
        else:
            @pl.when(when)
            def _():
                make().start()
        sent.append((make, when))

    def send(src, dst, send_sem, recv_sem, peer, when=None):
        start(lambda: (src, dst, send_sem, recv_sem, peer), when)

    def arrived(dst, sem):
        pltpu.make_async_copy(dst, dst, sem).wait()

    def far(o, when):
        send(seen.at[s, t], seen.at[s, t], far_send.at[o], seen_sem.at[s, t], (o, q, 0), when)

    own.wait()
    for o in range(n_s - 1):
        for p in range(n_t):
            @pl.when((o < s) & (t == 0))
            def _():
                signal(in_s.at[s], (o, q, p))
    for p in range(n_t - 1):
        @pl.when(p < t)
        def _():
            signal(in_t.at[t], (s, q, p))
    for o in range(n_q - 1):
        for p in range(n_t):
            @pl.when((o < q) & ((t == last) | (p == last)))
            def _():
                signal(in_q.at[q, t], (s, o, p))
    for o in range(n_s - 2):
        far(o, (o < s) & (s < n_s - 1))
    far(n_s - 2, s == n_s - 1)
    for p in range(n_t):
        @pl.when(p > t)
        def _():
            pl.semaphore_wait(in_t.at[p], 1)
        send(seen.at[s, t], seen.at[s, t], chip_send.at[p], seen_sem.at[s, t], (s, q, p), p != t)
    @pl.when(s == n_s - 1)
    def _():
        for p in range(n_t):
            @pl.when(p != t)
            def _():
                arrived(seen.at[s, p], seen_sem.at[s, p])
    if n_s > 2:
        far(0, s == n_s - 1)

    def upward():
        for o in range(1, n_s):
            @pl.when(o > s)
            def _():
                pl.semaphore_wait(in_s.at[o], 1)
            far(o, o > s)

    def project(stage):
        for k in plan[stage]:
            if k > 0:
                sec = section_of(k)
                @pl.when(t == 0)
                def _():
                    for p in range(n_t):
                        arrived(seen.at[sec, p], seen_sem.at[sec, p])
                for o in range(1, n_t):
                    send(
                        seen.at[sec],
                        seen.at[sec],
                        pass_send.at[k, 0, o],
                        seen_sem.at[sec, 0],
                        (s, q, o),
                        t == 0,
                    )

                @pl.when(t != 0)
                def _():
                    arrived(seen.at[sec], seen_sem.at[sec, 0])
            else:
                for p in range(n_t):
                    @pl.when((p != t) & (s < n_s - 1))
                    def _():
                        arrived(seen.at[s, p], seen_sem.at[s, p])
        if stage == 0:
            load.wait()
        parts = [
            seen[section_of(k) if k else s].reshape(n_t * shard, seen.shape[3])
            for k in plan[stage]
        ]
        share = len(parts) * part
        first = plan[stage][0] * part
        rows_at = pl.ds(first, share)
        block = parts[0] if len(parts) == 1 else jnp.concatenate(parts, 0)
        me = lax.rem(q, groups)
        for down, up in zip(range(groups - 1, -1, -1), [*range(1, groups), 0]):
            g = jnp.where(t == 0, partner(me, down, groups), partner(me, up, groups))
            at = pl.ds(pl.multiple_of(g * width, width), width)
            product = jnp.dot(block, weights[:, at], preferred_element_type=jnp.float32)
            for b in range(blocks):
                o = b * groups + g
                partial[o, rows_at] = product[b * share : (b + 1) * share]
                if stage == 0:
                    @pl.when(o > q)
                    def _():
                        pl.semaphore_wait(in_q.at[o, last], 1)
                send(
                    partial.at[o, rows_at],
                    landed.at[t, q, rows_at],
                    sum_send.at[stage, o],
                    sum_recv.at[stage, t, q],
                    (s, o, last),
                    (o != q) | (t != last),
                )

    def span(bundle):
        first = plan[bundle[0]][0] * part
        return first, sum(len(plan[stage]) for stage in bundle) * part

    def place(bundle, o):
        share = span(bundle)[1]
        row = plan[bundle[0]][0] * n_t * shard + (o // groups) * share
        if not isinstance(o, int):
            row = pl.multiple_of(row, share)
        return pl.ds(o % groups * each, each), pl.ds(row, share)

    others = [partner(q, k, n_q) if groups == n_q else lax.rem(q + k, n_q) for k in range(n_q)]
    mine_at = [place(bundle, q) for bundle in bundles]

    def finish(stage):
        own_at = pl.ds(plan[stage][0] * part, len(plan[stage]) * part)
        for p in range(n_t):
            for k in range(n_q):
                o = lax.rem(q + k, n_q)
                if p != last or k > 0:
                    arrived(landed.at[p, o, own_at], sum_recv.at[stage, p, o])
            for h in range(each):
                at_k = slice(2 * h * head_dim, (2 * h + 1) * head_dim)
                at_v = slice((2 * h + 1) * head_dim, (2 * h + 2) * head_dim)
                mine = partial.at[q] if p == last else landed.at[p, q]
                raw_k, raw_v = mine[own_at, at_k], mine[own_at, at_v]
                for k in range(1, n_q):
                    o = lax.rem(q + k, n_q)
                    raw_k += landed[p, o, own_at, at_k]
                    raw_v += landed[p, o, own_at, at_v]
                mean = jnp.mean(raw_k * raw_k, axis=-1, keepdims=True)
                scaled = raw_k * lax.rsqrt(mean + eps_norm) * gain[...]
                ready[p, h, 0, own_at] = scaled.astype(jnp.bfloat16)
                ready[p, h, 1, own_at] = raw_v.astype(jnp.bfloat16)
            closing = [b for b, bundle in enumerate(bundles) if bundle[-1] == stage]
            for b in closing:
                deliver(b, p)

    def deliver(b, p):
        heads_at, rows_at = mine_at[b]
        sent_at = pl.ds(*span(bundles[b]))
        for k in range(n_q - 1, -1, -1):
            if k == 0 and p == last:
                kv_ref[heads_at, :, rows_at, :] = ready[p, :, :, sent_at]
                continue
            o = others[k]
            if b == 0 and p != last and k > 0:
                @pl.when(o > q)
                def _():
                    pl.semaphore_wait(in_q.at[o, p], 1)
            start(
                lambda p=p, o=o: (
                    ready.at[p, :, :, sent_at],
                    kv_ref.at[heads_at, :, rows_at, :],
                    kv_send.at[b, p, o],
                    kv_recv.at[b, q],
                    (s, o, p),
                )
            )

    def owner(step):
        before = len(sent)

        @pl.when(t == last)
        def _():
            step()
        sent[before:] = [(make, t == last) for make, _ in sent[before:]]

    def collect(b, o):
        heads_at, rows_at = place(bundles[b], o)

        @pl.when((o != q) | (t != last))
        def _():
            arrived(kv_ref.at[heads_at, :, rows_at, :], kv_recv.at[b, o])

    def attend_early(j):
        def done(i, g, result):
            at = ((j * each + i) * group + g) * head_dim
            early_ref[0, :, at : at + pair * head_dim] = result

        first_head = partner(lax.rem(q, groups), early[j], groups) * each
        heads = [first_head + i for i in range(each)]
        attention(group, pair, staged_ref, kv_ref, gate, heads, done)

    load_gain.wait()
    upward()
    for stage in range(stages):
        project(stage)
        if stage == 0:
            for o in range(1, n_s - 2):
                far(o, s == n_s - 1)
        if stage >= 2:
            owner(functools.partial(finish, stage - 2))
    for stage in range(max(stages - 2, 0), stages):
        owner(functools.partial(finish, stage))
    stage_queries.wait()
    load_gate.wait()
    for j in range(len(early)):
        for b in range(len(bundles)):
            collect(b, others[early[j]])
        attend_early(j)
    for k in range(n_q):
        if k not in early:
            for b in range(len(bundles)):
                collect(b, others[k])
    for make, when in sent:
        if when is None:
            make().wait_send()
        else:
            @pl.when(when)
            def _():
                make().wait_send()


def local(sizes, queries, vision, kv_weight, key_gain, head_gate):
    n_s, n_q, n_t = sizes
    head_dim = key_gain.shape[1]
    shard, features = vision.shape
    columns = kv_weight.shape[2]
    rows = shard * n_s * n_t
    inner = columns // (2 * head_dim)
    blocks = n_q // math.gcd(inner, n_q)
    step = max(n_s // 4, 1)
    while step < n_s and step * n_t * shard % (16 * blocks):
        step += 1
    cuts = [k for k in (0, step, 2 * step) if k < n_s] + [n_s]
    plan = [list(range(a, b)) for a, b in zip(cuts, cuts[1:])]
    stages = len(plan)
    bundles = [list(range(stages - 1)), [stages - 1]] if blocks == 1 else [[i] for i in range(stages)]
    each = inner // math.gcd(inner, n_q)
    hbm = pl.BlockSpec(memory_space=pltpu.HBM)
    vmem = pl.BlockSpec(memory_space=pltpu.VMEM)
    dma = pltpu.SemaphoreType.DMA
    regular = pltpu.SemaphoreType.REGULAR
    heads = head_gate.shape[1]
    group = heads // inner
    pair = 2 if group % 2 == 0 and rows == head_dim else 1
    groups = n_q // blocks
    early = (0,) if blocks == 1 else ()
    late = tuple(k for k in range(groups) if k not in early)
    ahead = [pltpu.VMEM(queries.shape[:2] + (len(early) * each * group * head_dim,), jnp.bfloat16)]
    ahead = ahead if early else []
    smem = pl.BlockSpec(memory_space=pltpu.SMEM)
    kv, staged, *ahead = pl.pallas_call(
        functools.partial(project_kernel, sizes, plan, bundles, group, pair, early),
        out_shape=(
            pltpu.VMEM((inner, 2, rows, head_dim), jnp.bfloat16),
            pltpu.VMEM(queries.shape, jnp.bfloat16),
            *ahead,
        ),
        in_specs=[hbm] * 5,
        out_specs=(vmem, vmem) + (vmem,) * len(ahead),
        scratch_shapes=[
            pltpu.VMEM((n_s, n_t, shard, features), jnp.bfloat16),
            pltpu.VMEM((features, columns), jnp.bfloat16),
            pltpu.VMEM(key_gain.shape, jnp.float32),
            pltpu.VMEM((n_q, rows // blocks, each * 2 * head_dim), jnp.float32),
            pltpu.VMEM((n_t, n_q, rows // blocks, each * 2 * head_dim), jnp.float32),
            pltpu.VMEM((n_t, each, 2, rows // blocks, head_dim), jnp.bfloat16),
            pltpu.SMEM(head_gate.shape, jnp.float32),
            dma((5,)),
            dma((n_s,)),
            dma((n_t,)),
            dma((n_s, n_t, n_t)),
            dma((n_s, n_t)),
            dma((stages, n_q)),
            dma((stages, n_t, n_q)),
            dma((stages, n_t, n_q)),
            dma((stages, n_q)),
            regular((n_s,)),
            regular((n_q, n_t)),
            regular((n_t,)),
        ],
        compiler_params=pltpu.CompilerParams(
            collective_id=0, has_side_effects=True, vmem_limit_bytes=24 << 20
        ),
        name="project",
    )(
        *[
            pltpu.with_memory_space_constraint(x, pltpu.HBM)
            for x in (vision, kv_weight, key_gain, queries, head_gate)
        ]
    )

    return pl.pallas_call(
        functools.partial(attend_kernel, group, pair, early, late),
        out_shape=jax.ShapeDtypeStruct(queries.shape, jnp.bfloat16),
        in_specs=[vmem, vmem, smem] + [vmem] * len(ahead),
        out_specs=hbm,
        scratch_shapes=[
            pltpu.VMEM(queries.shape[:2] + (len(late) * each * group * head_dim,), jnp.bfloat16),
            dma((len(early) + len(late) * each * group // pair,)),
        ],
        compiler_params=pltpu.CompilerParams(vmem_limit_bytes=24 << 20),
        name="attend",
    )(staged, kv, head_gate, *ahead)


def solution(mesh):
    sizes = tuple(mesh.shape[name] for name in ("section", "seq", "tp"))
    return jax.shard_map(
        functools.partial(local, sizes),
        mesh=mesh,
        in_specs=(
            P("section", "seq", "tp"),
            P(("section", "tp"), "seq"),
            P("section", "seq", "tp"),
            P("section", None),
            P("section", "tp"),
        ),
        out_specs=P("section", "seq", "tp"),
        check_vma=False,
    )
```

```python
import functools
import math

import jax
import jax.numpy as jnp
from jax import lax
from jax.experimental import pallas as pl
from jax.experimental.pallas import tpu as pltpu
from jax.sharding import PartitionSpec as P

MESH = pl.DeviceIdType.MESH
eps_norm = 1e-05


def partner(i, k, n):
    if n & (n - 1):
        return lax.rem(i + k, n)
    result, bit = i, 1
    while bit < n:
        if k & bit:
            result = result + bit - 2 * bit * ((i // bit) % 2)
        bit *= 2
    return result


def attention(group, pair, q_ref, kv_ref, gate_ref, heads, done):
    _, _, rows, head_dim = kv_ref.shape
    scale = head_dim ** (-0.5)

    def diagonal(block):
        if pair == 1:
            return block
        zero = jnp.zeros_like(block)
        return jnp.concatenate(
            [jnp.concatenate([block, zero], 1), jnp.concatenate([zero, block], 1)], 0
        )

    ones = diagonal(jnp.ones((rows, head_dim), jnp.bfloat16))
    made = {}

    def block(i, kind):
        if (i, kind) not in made:
            made[i, kind] = diagonal(kv_ref[heads[i], kind])
        return made[i, kind]

    wide = pair * head_dim
    units = [(i, g) for i in range(len(heads)) for g in range(0, group, pair)]

    def score(i, g):
        start = pl.multiple_of(heads[i] * (group * head_dim) + g * head_dim, wide)
        return lax.dot_general(
            q_ref[0, :, pl.ds(start, wide)],
            block(i, 0),
            (((1,), (1,)), ((), ())),
            preferred_element_type=jnp.float32,
        )

    def soften(scores):
        exps = []
        for p in range(pair):
            part = scores[:, p * rows : (p + 1) * rows]
            peak = jnp.max(part, axis=-1, keepdims=True)
            exps.append(jnp.exp((part - peak) * scale).astype(jnp.bfloat16))
        return exps[0] if pair == 1 else jnp.concatenate(exps, 1)

    def mix(exps, i, g):
        gates = [
            jnp.full((1, head_dim), gate_ref[0, heads[i] * group + g + p]) for p in range(pair)
        ]
        gates = gates[0] if pair == 1 else jnp.concatenate(gates, 1)
        mixed = jnp.dot(exps, block(i, 1), preferred_element_type=jnp.float32)
        total = jnp.dot(exps, ones, preferred_element_type=jnp.float32)
        result = mixed / total * jnp.tanh(gates)
        done(i, g, result.astype(jnp.bfloat16))

    depth = 3
    waiting_scores, waiting_exps = [], []
    for step in range(len(units) + 2 * depth):
        if step < len(units):
            waiting_scores.append(score(*units[step]))
        if depth <= step < len(units) + depth:
            waiting_exps.append(soften(waiting_scores.pop(0)))
        if step >= 2 * depth:
            mix(waiting_exps.pop(0), *units[step - 2 * depth])


def attend_kernel(
    group, pair, early, late, q_ref, kv_ref, gate_ref, *rest
):
    early_ref = rest[0] if early else None
    out_hbm, out_ref, out_sem = rest[-3:]
    head_dim = kv_ref.shape[3]
    groups = len(early) + len(late)
    each = kv_ref.shape[0] // groups
    me = lax.rem(lax.axis_index("seq"), groups)
    copies = []

    def write(src, head, g, wide):
        start = pl.multiple_of(head * (group * head_dim) + g * head_dim, wide)
        copy = pltpu.make_async_copy(
            src, out_hbm.at[:, :, pl.ds(start, wide)], out_sem.at[len(copies)]
        )
        copy.start()
        copies.append(copy)

    block = each * group * head_dim
    for j, k in enumerate(early):
        write(early_ref.at[:, :, j * block : (j + 1) * block], partner(me, k, groups) * each, 0, block)
    heads = [partner(me, k, groups) * each + i for k in late for i in range(each)]
    wide = pair * head_dim

    def done(i, g, result):
        at = slice((i * group + g) * head_dim, (i * group + g) * head_dim + wide)
        out_ref[0, :, at] = result
        write(out_ref.at[:, :, at], heads[i], g, wide)

    attention(group, pair, q_ref, kv_ref, gate_ref, heads, done)
    for copy in copies:
        copy.wait()


def project_kernel(
    sizes,
    plan,
    bundles,
    group,
    pair,
    early,
    vision_ref,
    weight_ref,
    gain_ref,
    query_ref,
    gate_ref,
    kv_ref,
    staged_ref,
    *rest,
):
    early_ref = rest[0] if early else None
    scratch = rest[1:] if early else rest
    return project_steps(
        sizes, plan, bundles, group, pair, early, vision_ref, weight_ref, gain_ref, query_ref, gate_ref,
        kv_ref, staged_ref, early_ref, *scratch
    )


def project_steps(
    sizes,
    plan,
    bundles,
    group,
    pair,
    early,
    vision_ref,
    weight_ref,
    gain_ref,
    query_ref,
    gate_ref,
    kv_ref,
    staged_ref,
    early_ref,
    seen,
    weights,
    gain,
    partial,
    landed,
    ready,
    gate,
    load_sem,
    far_send,
    chip_send,
    pass_send,
    seen_sem,
    sum_send,
    sum_recv,
    kv_send,
    kv_recv,
    in_s,
    in_q,
    in_t,
):
    n_s, n_q, n_t = sizes
    s, q, t = lax.axis_index("section"), lax.axis_index("seq"), lax.axis_index("tp")
    inner, head_dim = kv_ref.shape[0], kv_ref.shape[3]
    stages = len(plan)
    shard = seen.shape[2]
    groups = math.gcd(inner, n_q)
    each = inner // groups
    blocks = n_q // groups
    part = n_t * shard // blocks
    width = each * 2 * head_dim
    half = n_s // 2 if n_s % 2 == 0 else n_s
    last = n_t - 1

    def section_of(k):
        base = (s // half) * half
        return lax.rem(base + (k // half) * half, n_s) + lax.rem(s + k, half)

    def at_device(peer):
        return tuple(0 * s + c if isinstance(c, int) else c for c in peer)

    def signal(sem, peer):
        pl.semaphore_signal(sem, inc=1, device_id=at_device(peer), device_id_type=MESH)

    own = pltpu.make_async_copy(vision_ref, seen.at[s, t], load_sem.at[0])
    load = pltpu.make_async_copy(weight_ref.at[0], weights, load_sem.at[1])
    load_gain = pltpu.make_async_copy(gain_ref, gain, load_sem.at[2])
    stage_queries = pltpu.make_async_copy(query_ref, staged_ref, load_sem.at[3])
    load_gate = pltpu.make_async_copy(gate_ref, gate, load_sem.at[4])

    barrier = pltpu.get_barrier_semaphore()
    for o in range(1, n_s):
        for p in range(n_t):
            @pl.when((o > s) & ((t == 0) | (p == 0)))
            def _():
                signal(barrier, (o, q, p))
    for o in range(1, n_q):
        for p in range(n_t):
            @pl.when((o > q) & ((t == last) | (p == last)))
            def _():
                signal(barrier, (s, o, p))
    for p in range(1, n_t):
        @pl.when(p > t)
        def _():
            signal(barrier, (s, q, p))
    own.start()
    load.start()
    load_gain.start()
    load_gate.start()
    stage_queries.start()
    earlier = s * jnp.where(t == 0, n_t, 1) + q * jnp.where(t == last, n_t, 1) + t

    @pl.when(earlier > 0)
    def _():
        pl.semaphore_wait(barrier, earlier)

    sent = []

    def start(build, when=None):
        def make():
            src, dst, send_sem, recv_sem, peer = build()
            return pltpu.make_async_remote_copy(
                src_ref=src,
                dst_ref=dst,
                send_sem=send_sem,
                recv_sem=recv_sem,
                device_id=at_device(peer),
                device_id_type=MESH,
            )

        if when is None:
            make().start()
        else:
            @pl.when(when)
            def _():
                make().start()
        sent.append((make, when))

    def send(src, dst, send_sem, recv_sem, peer, when=None):
        start(lambda: (src, dst, send_sem, recv_sem, peer), when)

    def arrived(dst, sem):
        pltpu.make_async_copy(dst, dst, sem).wait()

    def far(o, when):
        send(seen.at[s, t], seen.at[s, t], far_send.at[o], seen_sem.at[s, t], (o, q, 0), when)

    own.wait()
    for o in range(n_s - 1):
        for p in range(n_t):
            @pl.when((o < s) & (t == 0))
            def _():
                signal(in_s.at[s], (o, q, p))
    for p in range(n_t - 1):
        @pl.when(p < t)
        def _():
            signal(in_t.at[t], (s, q, p))
    for o in range(n_q - 1):
        for p in range(n_t):
            @pl.when((o < q) & ((t == last) | (p == last)))
            def _():
                signal(in_q.at[q, t], (s, o, p))
    for o in range(n_s - 2):
        far(o, (o < s) & (s < n_s - 1))
    far(n_s - 2, s == n_s - 1)
    for p in range(n_t):
        @pl.when(p > t)
        def _():
            pl.semaphore_wait(in_t.at[p], 1)
        send(seen.at[s, t], seen.at[s, t], chip_send.at[p], seen_sem.at[s, t], (s, q, p), p != t)
    @pl.when(s == n_s - 1)
    def _():
        for p in range(n_t):
            @pl.when(p != t)
            def _():
                arrived(seen.at[s, p], seen_sem.at[s, p])
    if n_s > 2:
        far(0, s == n_s - 1)

    def upward(near):
        for d in range(1, n_s):
            if (d == 1) == near:
                @pl.when(s + d < n_s)
                def _():
                    pl.semaphore_wait(in_s.at[s + d], 1)
                far(s + d, s + d < n_s)

    def project(stage):
        for k in plan[stage]:
            if k > 0:
                sec = section_of(k)
                @pl.when(t == 0)
                def _():
                    for p in range(n_t):
                        arrived(seen.at[sec, p], seen_sem.at[sec, p])
                for o in range(1, n_t):
                    send(
                        seen.at[sec],
                        seen.at[sec],
                        pass_send.at[k, 0, o],
                        seen_sem.at[sec, 0],
                        (s, q, o),
                        t == 0,
                    )

                @pl.when(t != 0)
                def _():
                    arrived(seen.at[sec], seen_sem.at[sec, 0])
            else:
                for p in range(n_t):
                    @pl.when((p != t) & (s < n_s - 1))
                    def _():
                        arrived(seen.at[s, p], seen_sem.at[s, p])
        if stage == 0:
            load.wait()
        parts = [
            seen[section_of(k) if k else s].reshape(n_t * shard, seen.shape[3])
            for k in plan[stage]
        ]
        share = len(parts) * part
        first = plan[stage][0] * part
        rows_at = pl.ds(first, share)
        block = parts[0] if len(parts) == 1 else jnp.concatenate(parts, 0)
        me = lax.rem(q, groups)
        for down, up in zip(range(groups - 1, -1, -1), [*range(1, groups), 0]):
            g = jnp.where(t == 0, partner(me, down, groups), partner(me, up, groups))
            at = pl.ds(pl.multiple_of(g * width, width), width)
            product = jnp.dot(block, weights[:, at], preferred_element_type=jnp.float32)
            for b in range(blocks):
                o = b * groups + g
                partial[o, rows_at] = product[b * share : (b + 1) * share]
                if stage == 0:
                    @pl.when(o > q)
                    def _():
                        pl.semaphore_wait(in_q.at[o, last], 1)
                send(
                    partial.at[o, rows_at],
                    landed.at[t, q, rows_at],
                    sum_send.at[stage, o],
                    sum_recv.at[stage, t, q],
                    (s, o, last),
                    (o != q) | (t != last),
                )

    def span(bundle):
        first = plan[bundle[0]][0] * part
        return first, sum(len(plan[stage]) for stage in bundle) * part

    def place(bundle, o):
        share = span(bundle)[1]
        row = plan[bundle[0]][0] * n_t * shard + (o // groups) * share
        if not isinstance(o, int):
            row = pl.multiple_of(row, share)
        return pl.ds(o % groups * each, each), pl.ds(row, share)

    others = [partner(q, k, n_q) if groups == n_q else lax.rem(q + k, n_q) for k in range(n_q)]
    mine_at = [place(bundle, q) for bundle in bundles]

    def finish(stage):
        own_at = pl.ds(plan[stage][0] * part, len(plan[stage]) * part)
        for p in range(n_t):
            for k in range(n_q):
                o = lax.rem(q + k, n_q)
                if p != last or k > 0:
                    arrived(landed.at[p, o, own_at], sum_recv.at[stage, p, o])
            for h in range(each):
                at_k = slice(2 * h * head_dim, (2 * h + 1) * head_dim)
                at_v = slice((2 * h + 1) * head_dim, (2 * h + 2) * head_dim)
                mine = partial.at[q] if p == last else landed.at[p, q]
                raw_k, raw_v = mine[own_at, at_k], mine[own_at, at_v]
                for k in range(1, n_q):
                    o = lax.rem(q + k, n_q)
                    raw_k += landed[p, o, own_at, at_k]
                    raw_v += landed[p, o, own_at, at_v]
                mean = jnp.mean(raw_k * raw_k, axis=-1, keepdims=True)
                scaled = raw_k * lax.rsqrt(mean + eps_norm) * gain[...]
                ready[p, h, 0, own_at] = scaled.astype(jnp.bfloat16)
                ready[p, h, 1, own_at] = raw_v.astype(jnp.bfloat16)
            closing = [b for b, bundle in enumerate(bundles) if bundle[-1] == stage]
            for b in closing:
                deliver(b, p)

    def deliver(b, p):
        heads_at, rows_at = mine_at[b]
        sent_at = pl.ds(*span(bundles[b]))
        for k in range(n_q - 1, -1, -1):
            if k == 0 and p == last:
                kv_ref[heads_at, :, rows_at, :] = ready[p, :, :, sent_at]
                continue
            o = others[k]
            if b == 0 and p != last and k > 0:
                @pl.when(o > q)
                def _():
                    pl.semaphore_wait(in_q.at[o, p], 1)
            start(
                lambda p=p, o=o: (
                    ready.at[p, :, :, sent_at],
                    kv_ref.at[heads_at, :, rows_at, :],
                    kv_send.at[b, p, o],
                    kv_recv.at[b, q],
                    (s, o, p),
                )
            )

    def owner(step):
        before = len(sent)

        @pl.when(t == last)
        def _():
            step()
        sent[before:] = [(make, t == last) for make, _ in sent[before:]]

    def collect(b, o):
        heads_at, rows_at = place(bundles[b], o)

        @pl.when((o != q) | (t != last))
        def _():
            arrived(kv_ref.at[heads_at, :, rows_at, :], kv_recv.at[b, o])

    def attend_early(j):
        def done(i, g, result):
            at = ((j * each + i) * group + g) * head_dim
            early_ref[0, :, at : at + pair * head_dim] = result

        first_head = partner(lax.rem(q, groups), early[j], groups) * each
        heads = [first_head + i for i in range(each)]
        attention(group, pair, staged_ref, kv_ref, gate, heads, done)

    load_gain.wait()
    upward(True)
    for stage in range(stages):
        project(stage)
        if stage == 0:
            upward(False)
            for o in range(1, n_s - 2):
                far(o, s == n_s - 1)
        if stage >= 2:
            owner(functools.partial(finish, stage - 2))
    for stage in range(max(stages - 2, 0), stages):
        owner(functools.partial(finish, stage))
    stage_queries.wait()
    load_gate.wait()
    for j in range(len(early)):
        for b in range(len(bundles)):
            collect(b, others[early[j]])
        attend_early(j)
    for k in range(n_q):
        if k not in early:
            for b in range(len(bundles)):
                collect(b, others[k])
    for make, when in sent:
        if when is None:
            make().wait_send()
        else:
            @pl.when(when)
            def _():
                make().wait_send()


def local(sizes, queries, vision, kv_weight, key_gain, head_gate):
    n_s, n_q, n_t = sizes
    head_dim = key_gain.shape[1]
    shard, features = vision.shape
    columns = kv_weight.shape[2]
    rows = shard * n_s * n_t
    inner = columns // (2 * head_dim)
    blocks = n_q // math.gcd(inner, n_q)
    step = max(n_s // 4, 1)
    while step < n_s and step * n_t * shard % (16 * blocks):
        step += 1
    cuts = [k for k in (0, step, 2 * step) if k < n_s] + [n_s]
    plan = [list(range(a, b)) for a, b in zip(cuts, cuts[1:])]
    stages = len(plan)
    bundles = [list(range(stages - 1)), [stages - 1]] if blocks == 1 else [[i] for i in range(stages)]
    each = inner // math.gcd(inner, n_q)
    hbm = pl.BlockSpec(memory_space=pltpu.HBM)
    vmem = pl.BlockSpec(memory_space=pltpu.VMEM)
    dma = pltpu.SemaphoreType.DMA
    regular = pltpu.SemaphoreType.REGULAR
    heads = head_gate.shape[1]
    group = heads // inner
    pair = 2 if group % 2 == 0 and rows == head_dim else 1
    groups = n_q // blocks
    early = (0,) if blocks == 1 else ()
    late = tuple(k for k in range(groups) if k not in early)
    ahead = [pltpu.VMEM(queries.shape[:2] + (len(early) * each * group * head_dim,), jnp.bfloat16)]
    ahead = ahead if early else []
    smem = pl.BlockSpec(memory_space=pltpu.SMEM)
    kv, staged, *ahead = pl.pallas_call(
        functools.partial(project_kernel, sizes, plan, bundles, group, pair, early),
        out_shape=(
            pltpu.VMEM((inner, 2, rows, head_dim), jnp.bfloat16),
            pltpu.VMEM(queries.shape, jnp.bfloat16),
            *ahead,
        ),
        in_specs=[hbm] * 5,
        out_specs=(vmem, vmem) + (vmem,) * len(ahead),
        scratch_shapes=[
            pltpu.VMEM((n_s, n_t, shard, features), jnp.bfloat16),
            pltpu.VMEM((features, columns), jnp.bfloat16),
            pltpu.VMEM(key_gain.shape, jnp.float32),
            pltpu.VMEM((n_q, rows // blocks, each * 2 * head_dim), jnp.float32),
            pltpu.VMEM((n_t, n_q, rows // blocks, each * 2 * head_dim), jnp.float32),
            pltpu.VMEM((n_t, each, 2, rows // blocks, head_dim), jnp.bfloat16),
            pltpu.SMEM(head_gate.shape, jnp.float32),
            dma((5,)),
            dma((n_s,)),
            dma((n_t,)),
            dma((n_s, n_t, n_t)),
            dma((n_s, n_t)),
            dma((stages, n_q)),
            dma((stages, n_t, n_q)),
            dma((stages, n_t, n_q)),
            dma((stages, n_q)),
            regular((n_s,)),
            regular((n_q, n_t)),
            regular((n_t,)),
        ],
        compiler_params=pltpu.CompilerParams(
            collective_id=0, has_side_effects=True, vmem_limit_bytes=24 << 20
        ),
        name="project",
    )(
        *[
            pltpu.with_memory_space_constraint(x, pltpu.HBM)
            for x in (vision, kv_weight, key_gain, queries, head_gate)
        ]
    )

    return pl.pallas_call(
        functools.partial(attend_kernel, group, pair, early, late),
        out_shape=jax.ShapeDtypeStruct(queries.shape, jnp.bfloat16),
        in_specs=[vmem, vmem, smem] + [vmem] * len(ahead),
        out_specs=hbm,
        scratch_shapes=[
            pltpu.VMEM(queries.shape[:2] + (len(late) * each * group * head_dim,), jnp.bfloat16),
            dma((len(early) + len(late) * each * group // pair,)),
        ],
        compiler_params=pltpu.CompilerParams(vmem_limit_bytes=24 << 20),
        name="attend",
    )(staged, kv, head_gate, *ahead)


def solution(mesh):
    sizes = tuple(mesh.shape[name] for name in ("section", "seq", "tp"))
    return jax.shard_map(
        functools.partial(local, sizes),
        mesh=mesh,
        in_specs=(
            P("section", "seq", "tp"),
            P(("section", "tp"), "seq"),
            P("section", "seq", "tp"),
            P("section", None),
            P("section", "tp"),
        ),
        out_specs=P("section", "seq", "tp"),
        check_vma=False,
    )
```
